128 devices in a mesh: pipe: 4 (over z), head: 32 (over y, x, core).
Axes of the slice: x: 4, y: 4, z: 4, core: 2. Of those that a mesh axis runs over, the one named last changes fastest.
Arguments:
- hidden: bfloat16 [2, 64, 8192], P(None, 'head'), may hold values from -6 to 6
- norm_gain: float32 [4, 8192], P('pipe'), may hold values from 0.1 to 1.9
- w_x: bfloat16 [4, 8192, 16384], P('pipe', None, 'head'), may hold values from -0.0625 to 0.0625
- w_bc: bfloat16 [4, 8192, 4096], P('pipe', None, 'head'), may hold values from -0.03125 to 0.03125
- w_dt: bfloat16 [4, 8192, 256], P('pipe', None, 'head'), may hold values from -0.0625 to 0.0625
- conv_x: float32 [4, 4, 16384], P('pipe', None, 'head'), may hold values from -3 to 3
- conv_bc: float32 [4, 4, 4096], P('pipe'), may hold values from -3 to 3
- dt_bias: float32 [4, 256], P('pipe', 'head'), may hold values from -3 to 0.5
- a_rate: float32 [4, 256], P('pipe', 'head'), may hold values from 0.002 to 0.2
- d_skip: float32 [4, 256], P('pipe', 'head'), may hold values from 0.5 to 1.5
- w_out: bfloat16 [4, 16384, 8192], P('pipe', 'head'), may hold values from -0.046875 to 0.046875
- ssm_init: float32 [4, 256, 64, 256], P('pipe', 'head'), may hold values from -0.6 to 0.6
- conv_x_init: float32 [4, 3, 16384], P('pipe', None, 'head'), may hold values from -6 to 6
- conv_bc_init: float32 [4, 3, 4096], P('pipe'), may hold values from -3 to 3
Outputs:
- segment_out: bfloat16 [4, 2, 64, 8192], P('pipe', None, 'head')
- state_out: float32 [4, 256, 64, 256], P('pipe', 'head')
The draws below stay inside these ranges and needn't reach their ends.
All inputs are finite; a program needn't handle non-finite values.
Results may differ from the reference program's by a relative error of at most 0.039.
Values may be sent and summed in bfloat16 or wider, within the bound.
A program may use at most 128 MiB of HBM per device.

```python
import math
import jax
import jax.numpy as jnp
from jax import lax

D = 8192
HEADS = 256
HEAD_DIM = 64
STATE = 256
GROUPS = 8
CONV = 4
BLOCK = 64
MICRO = 2
INNER = 16384
N_PIPE = 4
N_HEAD = 32


def level_of(own_key, dims, cuts, smallest, largest):
    factor_of, own = 1.0, jax.random.fold_in(own_key, 6)
    for position, shards_of in cuts:
        draws = jnp.exp(jax.random.uniform(jax.random.fold_in(own, position), (shards_of,), jnp.float32, smallest / len(cuts), largest / len(cuts)))
        factor_of = factor_of * jnp.repeat(draws, dims[position] // shards_of).reshape([-1 if axis == position else 1 for axis in range(len(dims))])
    return factor_of


def bell_draw(rng, dims, width, most, cuts=(), kind=jnp.bfloat16):
    level = level_of(rng, dims, cuts, -0.22, 0.18) if cuts else 1.0
    values = jax.random.normal(rng, dims, jnp.float32) * width * level
    return jnp.minimum(jnp.maximum(values, -most), most).astype(kind)


def setup_inputs(seed: int = 0) -> dict:
    arg_keys = jax.random.split(jax.random.key(seed), 15)
    return {
        "hidden": bell_draw(arg_keys[0], (MICRO, BLOCK, D), 1.0, 6.0, ((1, 32),)),
        "norm_gain": jnp.clip(1.0 + 0.18 * jax.random.normal(arg_keys[1], (N_PIPE, D), jnp.float32), 0.1, 1.9),
        "w_x": bell_draw(arg_keys[2], (N_PIPE, D, INNER), D ** -0.5, 0.0625, ((0, 4), (2, 32))),
        "w_bc": bell_draw(arg_keys[3], (N_PIPE, D, 2 * GROUPS * STATE), (4 * D) ** -0.5, 0.03125, ((0, 4), (2, 32))),
        "w_dt": bell_draw(arg_keys[4], (N_PIPE, D, HEADS), D ** -0.5, 0.0625, ((0, 4), (2, 32))),
        "conv_x": bell_draw(arg_keys[5], (N_PIPE, CONV, INNER), CONV ** -0.5, 3.0, ((0, 4), (2, 32)), jnp.float32),
        "conv_bc": bell_draw(arg_keys[6], (N_PIPE, CONV, 2 * GROUPS * STATE), CONV ** -0.5, 3.0, ((0, 4),), jnp.float32),
        "dt_bias": jnp.clip(-3.0 + 3.5 * jax.random.uniform(arg_keys[7], (N_PIPE, HEADS), jnp.float32) ** level_of(arg_keys[7], (N_PIPE, HEADS), ((0, 4), (1, 32)), -0.2, 0.2), -3.0, 0.5),
        "a_rate": jnp.clip(jnp.exp(math.log(0.2) - 4.6051702 * jax.random.uniform(arg_keys[8], (N_PIPE, HEADS), jnp.float32) ** level_of(arg_keys[8], (N_PIPE, HEADS), ((0, 4), (1, 32)), -0.2, 0.2)), 0.002, 0.2),
        "d_skip": jnp.clip(0.5 + 1.0 * jax.random.uniform(arg_keys[9], (N_PIPE, HEADS), jnp.float32) ** level_of(arg_keys[9], (N_PIPE, HEADS), ((0, 4), (1, 32)), -0.2, 0.2), 0.5, 1.5),
        "w_out": bell_draw(arg_keys[10], (N_PIPE, INNER, D), INNER ** -0.5, 0.046875, ((0, 4), (1, 32))),
        "ssm_init": bell_draw(arg_keys[11], (N_PIPE, HEADS, HEAD_DIM, STATE), 0.1, 0.6, ((0, 4), (1, 32)), jnp.float32),
        "conv_x_init": bell_draw(arg_keys[12], (N_PIPE, CONV - 1, INNER), 1.0, 6.0, ((0, 4), (2, 32)), jnp.float32),
        "conv_bc_init": bell_draw(arg_keys[13], (N_PIPE, CONV - 1, 2 * GROUPS * STATE), 0.5, 3.0, ((0, 4),), jnp.float32),
    }


def rms_rows(block_in, norm_weight):
    floats = block_in.astype(jnp.float32)
    scaled = floats * lax.rsqrt(lax.optimization_barrier(jnp.mean(floats * floats, axis=-1, keepdims=True)) + 1e-05)
    return (scaled * norm_weight[None, :]).astype(jnp.bfloat16)

def causal_conv(tail_rows, values, taps):
    padded = jnp.concatenate([tail_rows, values], axis=0)
    length = values.shape[0]
    conv_sum = taps[0][None, :] * padded[0:length]
    for offset in range(1, taps.shape[0]):
        conv_sum = conv_sum + taps[offset][None, :] * padded[offset:offset + length]
    return (jax.nn.silu(conv_sum), padded[length:])

def scan_block(values, b_heads, c_heads, step_size, decay_rate, skip_gain, ssm_state):
    highest = lax.Precision.HIGHEST
    log_decay = jnp.cumsum(-step_size * decay_rate[None, :], axis=0)
    length = values.shape[0]
    causal = (jnp.arange(length)[:, None] >= jnp.arange(length)[None, :])[:, :, None]
    gap_log = log_decay[:, None, :] - log_decay[None, :, :]
    decay_pairs = jnp.where(causal, jnp.exp(jnp.where(causal, gap_log, 0.0)), 0.0)
    scores = jnp.einsum('thn,shn->tsh', c_heads, b_heads, precision=highest)
    pair_weight = scores * decay_pairs * step_size[None, :, :]
    within = jnp.einsum('tsh,shp->thp', pair_weight, values, precision=highest)
    carried = jnp.exp(log_decay)[:, :, None] * jnp.einsum('thn,hpn->thp', c_heads, ssm_state, precision=highest)
    mixed_out = within + carried + skip_gain[None, :, None] * values
    end_log = log_decay[-1]
    to_end = jnp.exp(end_log[None, :] - log_decay) * step_size
    new_state = jnp.exp(end_log)[:, None, None] * ssm_state + jnp.einsum('sh,shp,shn->hpn', to_end, values, b_heads, precision=highest)
    return (mixed_out, new_state)

def reference(hidden, norm_gain, w_x, w_bc, w_dt, conv_x, conv_bc, dt_bias, a_rate, d_skip, w_out, ssm_init, conv_x_init, conv_bc_init):
    group_of = jnp.arange(HEADS) // (HEADS // GROUPS)
    share = INNER // N_HEAD
    current = [hidden[block_index] for block_index in range(MICRO)]
    layer_outs = []
    layer_states = []
    for layer_index in range(N_PIPE):
        ssm_state = ssm_init[layer_index]
        tail_x = conv_x_init[layer_index]
        tail_bc = conv_bc_init[layer_index]
        produced = []
        for block_index in range(MICRO):
            block_in = current[block_index]
            normed = rms_rows(block_in, norm_gain[layer_index])
            x_proj = jnp.dot(normed, w_x[layer_index], preferred_element_type=jnp.float32)
            bc_proj = jnp.dot(normed, w_bc[layer_index], preferred_element_type=jnp.float32).astype(jnp.bfloat16)
            dt_raw = jnp.dot(normed, w_dt[layer_index], preferred_element_type=jnp.float32)
            x_conv, tail_x = causal_conv(tail_x, x_proj, conv_x[layer_index])
            bc_conv, tail_bc = causal_conv(tail_bc, bc_proj.astype(jnp.float32), conv_bc[layer_index])
            step_size = jax.nn.softplus(dt_raw + dt_bias[layer_index][None, :])
            grouped = bc_conv.reshape(BLOCK, 2, STATE, GROUPS)
            b_heads = jnp.transpose(grouped[:, 0][:, :, group_of], (0, 2, 1))
            c_heads = jnp.transpose(grouped[:, 1][:, :, group_of], (0, 2, 1))
            mixed, ssm_state = scan_block(x_conv.reshape(BLOCK, HEADS, HEAD_DIM), b_heads, c_heads, step_size, a_rate[layer_index], d_skip[layer_index], ssm_state)
            mixed_bf = mixed.reshape(BLOCK, INNER).astype(jnp.bfloat16)
            summed = jnp.zeros((BLOCK, D), jnp.float32)
            for part_index in range(N_HEAD):
                partial_value = jnp.dot(mixed_bf[:, part_index * share:(part_index + 1) * share], w_out[layer_index][part_index * share:(part_index + 1) * share], preferred_element_type=jnp.float32)
                rounded = lax.optimization_barrier(partial_value.astype(jnp.bfloat16))
                summed = summed + rounded.astype(jnp.float32)
            produced.append((block_in.astype(jnp.float32) + summed).astype(jnp.bfloat16))
        layer_outs.append(jnp.stack(produced, axis=0))
        layer_states.append(ssm_state)
        current = produced
    return (jnp.stack(layer_outs, axis=0), jnp.stack(layer_states, axis=0))
```

```python
import functools

import jax
import jax.numpy as jnp
from jax import lax
from jax.experimental import pallas as pl
from jax.experimental.pallas import tpu as pltpu
from jax.sharding import PartitionSpec as P

GROUPS = 8
STATE = 256
HEAD_DIM = 64
MESH = pl.DeviceIdType.MESH
F32 = jnp.float32
BF16 = jnp.bfloat16
AHEAD = 3


def dot(a, b, dims=((1,), (0,)), precision=None):
    return lax.dot_general(a, b, (dims, ((), ())), precision=precision, preferred_element_type=F32)


def exact(a, b):
    return dot(a, b, precision=lax.Precision.HIGHEST)


def section(
    sizes,
    hid,
    gain,
    w_x,
    w_bc,
    w_dt,
    w_out,
    ssm_in,
    taps,
    tails,
    dt_bias,
    a_rate,
    d_skip,
    out,
    state,
    wx_v,
    wbd_v,
    wdt_v,
    wo_v,
    ssm_v,
    ssm_t,
    h_all,
    first_in,
    acc,
    squares,
    padded,
    bc_send,
    bc_recv,
    y_v,
    x_end,
    b_end,
    decay_end,
    sib_send,
    sib_recv,
    sum_send,
    sum_recv,
    total,
    passed,
    out_send,
    load_sem,
    first_s,
    first_r,
    ag_s,
    ag_r,
    fwd_r,
    bc_s,
    bc_r,
    sib_s,
    sib_r,
    sum_s,
    sum_r,
    pass_s,
    pass_r,
    out_s,
    out_r,
    own_s,
):
    n_pipe, n_head, n_x, n_y = sizes
    n_chip = n_head // 2
    micro = hid.shape[0]
    rows = hid.shape[1]
    width = hid.shape[2]
    tokens = rows * n_head
    chunk = width // n_head
    inner = w_x.shape[2]
    heads = dt_bias.shape[1]
    bc_cols = w_bc.shape[2]
    per_group = n_head // GROUPS
    z = lax.axis_index("pipe")
    me = lax.axis_index("head")
    core = lax.rem(me, 2)
    chip = lax.div(me, 2)
    chip_x = lax.rem(chip, n_x)
    chip_y = lax.div(chip, n_x)
    sibling = chip * 2 + 1 - core

    def ahead(t):
        return lax.rem(chip_y + lax.div(t, n_x), n_y) * n_x + lax.rem(chip_x + lax.rem(t, n_x), n_x)

    def behind(t):
        return lax.rem(chip_y + n_y - lax.div(t, n_x), n_y) * n_x + lax.rem(
            chip_x + n_x - lax.rem(t, n_x), n_x
        )

    def remote(src, dst, send, recv, head, pipe=None):
        return pltpu.make_async_remote_copy(
            src_ref=src,
            dst_ref=dst,
            send_sem=send,
            recv_sem=recv,
            device_id={"pipe": z if pipe is None else pipe, "head": head},
            device_id_type=MESH,
        )

    def drain(ref, sem):
        pltpu.make_async_copy(ref, ref, sem).wait()

    def each(first, last, body):
        def step(t, carry):
            body(t)
            return carry

        lax.fori_loop(first, last, step, 0)

    def load_in(k):
        pltpu.make_async_copy(w_x.at[k], wx_v.at[k], load_sem.at[0]).start()
        pltpu.make_async_copy(w_bc.at[k], wbd_v.at[k, :, pl.ds(0, bc_cols)], load_sem.at[1]).start()

    each(0, n_chip, load_in)
    pltpu.make_async_copy(w_dt, wdt_v, load_sem.at[2]).start()
    pltpu.make_async_copy(ssm_in, ssm_v, load_sem.at[3]).start()
    for k in range(n_head):
        pltpu.make_async_copy(
            w_out.at[:, pl.ds(k * chunk, chunk)], wo_v.at[k], load_sem.at[4]
        ).start()

    barrier = pltpu.get_barrier_semaphore()

    def greet(t):
        pl.semaphore_signal(
            barrier,
            inc=1,
            device_id={"pipe": z, "head": lax.rem(me + t, n_head)},
            device_id_type=MESH,
        )

    each(1, n_head, greet)
    for other in (lax.rem(z + 1, n_pipe), lax.rem(z + n_pipe - 1, n_pipe)):
        pl.semaphore_signal(
            barrier, inc=1, device_id={"pipe": other, "head": me}, device_id_type=MESH
        )
    pl.semaphore_wait(barrier, n_head + 1)

    @pl.when(z == 0)
    def _():
        for m in range(micro):

            def give(t):
                to = lax.rem(me + t, n_head)
                remote(
                    hid.at[m, :, pl.ds(pl.multiple_of(to * chunk, chunk), chunk)],
                    first_in.at[m, me],
                    first_s.at[m],
                    first_r.at[m],
                    to,
                ).start()

            each(1, n_head, give)
            pltpu.make_async_copy(
                hid.at[m, :, pl.ds(pl.multiple_of(me * chunk, chunk), chunk)],
                first_in.at[m, me],
                own_s,
            ).start()
            drain(first_in.at[m, 0], own_s)

    def spread(m):
        mine = h_all.at[m, me]

        def give(t):
            remote(mine, mine, ag_s, ag_r.at[m, t], ahead(t) * 2 + core).start()

        each(1, n_chip, give)
        remote(mine, mine, ag_s, fwd_r.at[m, 0], sibling).start()

    def begin(m):
        drain(first_in.at[m, pl.ds(0, n_head - 1)], first_r.at[m])
        for i in range(n_head):
            total[pl.ds(i * rows, rows), :] = first_in[m, i].astype(F32)
        h_all[m, me] = total[...].astype(BF16)
        spread(m)

    @pl.when(z == 0)
    def _():
        begin(0)

    drain(wdt_v, load_sem.at[2])
    for_pad = jnp.zeros((2 * chunk, 256 - bc_cols - heads), BF16)

    def join(k):
        wbd_v[k, :, bc_cols:256] = jnp.concatenate([wdt_v[k], for_pad], axis=1)

    each(0, n_chip, join)
    drain(ssm_v, load_sem.at[3])
    ssm_t[...] = ssm_v[...].reshape(heads * HEAD_DIM, STATE).T
    padded[5:8, :] = tails[...]
    drain(wx_v, load_sem.at[0])
    drain(wbd_v.at[:, :, pl.ds(0, bc_cols)], load_sem.at[1])

    def block(m):
        @pl.when(jnp.logical_and(z == 0, m > 0))
        def _():
            begin(m)

        @pl.when(z > 0)
        def _():
            remote(passed.at[m], h_all.at[m, me], pass_s, pass_r.at[m], me).wait_recv()
            spread(m)

        acc[...] = jnp.zeros_like(acc)
        squares[...] = jnp.zeros_like(squares)

        def relay(t):
            got = h_all.at[m, behind(t) * 2 + core]
            copy = remote(got, got, ag_s, ag_r.at[m, t], sibling)
            copy.wait_recv()
            remote(got, got, ag_s, fwd_r.at[m, t], sibling).start()

        each(1, 1 + AHEAD, relay)

        def project(t):
            @pl.when(t + 1 + AHEAD < n_chip)
            def _():
                relay(t + 1 + AHEAD)

            src = behind(t)
            theirs = h_all.at[m, src * 2 + 1 - core]
            remote(theirs, theirs, ag_s, fwd_r.at[m, t], sibling).wait_recv()
            values = jnp.concatenate([h_all[m, src * 2], h_all[m, src * 2 + 1]], axis=1).astype(F32)
            sq = values * values
            part = sq[:, 0:128]
            for k in range(1, 2 * chunk // 128):
                part = part + sq[:, k * 128 : (k + 1) * 128]
            squares[...] += part
            scaled = (values * gain[src]).astype(BF16)
            acc[:, 0:inner] += dot(scaled, wx_v[src])
            acc[:, inner : inner + 256] += dot(scaled, wbd_v[src])

        each(0, n_chip, project)
        inv = lax.rsqrt(jnp.sum(squares[...], axis=1, keepdims=True) / width + 1e-05)

        bc_dt = acc[:, inner : inner + 256] * inv
        bc_bf = bc_dt[:, 0:bc_cols].astype(BF16)
        bc_wide = jnp.concatenate([bc_bf, jnp.zeros((128 - tokens, bc_cols), BF16)], axis=0)
        at_row = lax.broadcasted_iota(jnp.int32, (bc_cols, bc_cols), 0)
        at_col = lax.broadcasted_iota(jnp.int32, (bc_cols, bc_cols), 1)
        width_n = bc_cols // GROUPS
        wanted = lax.rem(at_row, width_n) * GROUPS + lax.div(at_row, width_n)
        order = jnp.where(at_col == wanted, 1.0, 0.0).astype(BF16)
        bc_send[...] = dot(order, bc_wide, ((1,), (1,))).astype(BF16).reshape(bc_send.shape)

        def give_bc(t):
            to = lax.rem(me + t, n_head)
            remote(
                bc_send.at[lax.div(to, per_group)], bc_recv.at[m, me], bc_s, bc_r.at[m], to
            ).start()

        each(1, n_head, give_bc)
        bc_recv[m, me] = bc_send[lax.div(me, per_group)]

        padded[8 : 8 + tokens, 0:inner] = acc[:, 0:inner] * inv

        def conv(lo, hi):
            summed = taps[0:1, lo:hi] * padded[5 : 5 + tokens, lo:hi]
            for k in range(1, 4):
                summed = summed + taps[k : k + 1, lo:hi] * padded[5 + k : 5 + k + tokens, lo:hi]
            return summed * lax.logistic(summed)

        x = conv(0, inner)
        raw = bc_dt[:, bc_cols : bc_cols + heads] + dt_bias[...]
        step = jnp.maximum(raw, 0.0) + jnp.log1p(jnp.exp(-jnp.abs(raw)))
        tri_row = lax.broadcasted_iota(jnp.int32, (tokens, tokens), 0)
        tri_col = lax.broadcasted_iota(jnp.int32, (tokens, tokens), 1)
        log_decay = exact(jnp.where(tri_row >= tri_col, 1.0, 0.0), -step * a_rate[...])
        head_row = lax.broadcasted_iota(jnp.int32, (heads, inner), 0)
        head_col = lax.div(lax.broadcasted_iota(jnp.int32, (heads, inner), 1), HEAD_DIM)
        of_head = jnp.where(head_row == head_col, 1.0, 0.0)
        skip8 = jnp.broadcast_to(d_skip[...], (8, heads))
        wide = exact(jnp.concatenate([step, log_decay, skip8], axis=0), of_head)
        step_w = wide[0:tokens]
        log_w = wide[tokens : 2 * tokens]
        skip_w = wide[2 * tokens : 2 * tokens + 1]
        at_t = lax.broadcasted_iota(jnp.int32, (tokens, inner), 0)
        at_s = lax.rem(lax.broadcasted_iota(jnp.int32, (tokens, inner), 1), HEAD_DIM)
        log_s = jnp.sum(jnp.where(at_t == at_s, log_w, 0.0), axis=0, keepdims=True)
        causal = at_t >= at_s
        pair = jnp.where(causal, jnp.exp(jnp.where(causal, log_w - log_s, 0.0)), 0.0)
        log_end = log_w[tokens - 1 : tokens]
        x_dt = x * step_w
        x_end[...] = (jnp.exp(log_end - log_w) * x_dt).astype(BF16)
        decay_end[0:1, :] = jnp.exp(log_end)

        drain(bc_recv.at[m, pl.ds(0, n_head - 1)], bc_r.at[m])
        both = bc_recv[m].reshape(2 * STATE, 128).astype(F32).T
        padded[8 : 8 + tokens, inner : inner + 2 * STATE] = both[0:tokens]
        bc = conv(inner, inner + 2 * STATE)
        padded[5:8, :] = padded[5 + tokens : 8 + tokens, :]
        b_v = bc[:, 0:STATE].astype(BF16)
        c_v = bc[:, STATE : 2 * STATE].astype(BF16)
        b_end[...] = b_v
        scores = dot(c_v, jnp.concatenate([b_v, b_v], axis=0), ((1,), (1,)))
        weight = (jnp.concatenate([scores] * (heads // 2), axis=1) * pair).astype(BF16)
        lane = lax.broadcasted_iota(jnp.int32, (tokens, 2 * HEAD_DIM), 1)
        within = []
        for k in range(heads // 2):
            cols = slice(k * 2 * HEAD_DIM, (k + 1) * 2 * HEAD_DIM)
            two = x_dt[:, cols]
            stacked = jnp.concatenate(
                [jnp.where(lane < HEAD_DIM, two, 0.0), jnp.where(lane < HEAD_DIM, 0.0, two)], axis=0
            ).astype(BF16)
            within.append(dot(weight[:, cols], stacked))
        carried = jnp.exp(log_w) * dot(c_v, ssm_t[...].astype(BF16))
        y_v[...] = (jnp.concatenate(within, axis=1) + carried + skip_w * x).astype(BF16)

        @pl.when(m == 0)
        def _():
            drain(wo_v, load_sem.at[4])

        def for_sibling(i):
            t = lax.rem(i + 1, n_chip)
            sib_send[t] = dot(y_v[...], wo_v[ahead(t) * 2 + 1 - core]).astype(BF16)
            remote(sib_send.at[t], sib_recv.at[m, t], sib_s, sib_r.at[m, t], sibling).start()

        each(0, n_chip, for_sibling)

        def chip_sum(t):
            part = dot(y_v[...], wo_v[ahead(t) * 2 + core]).astype(BF16).astype(F32)
            remote(
                sib_send.at[t], sib_recv.at[m, t], sib_s, sib_r.at[m, t], sibling
            ).wait_recv()
            return part + sib_recv[m, t].astype(F32)

        def for_owner(t):
            sum_send[t] = chip_sum(t).astype(BF16)
            remote(
                sum_send.at[t],
                sum_recv.at[m, t],
                sum_s,
                sum_r.at[m, t],
                ahead(t) * 2 + core,
            ).start()

        each(1, n_chip, for_owner)
        total[...] = chip_sum(0) + h_all[m, me].astype(F32)

        ssm_t[...] = decay_end[0:1, :] * ssm_t[...] + dot(b_end[...], x_end[...], ((0,), (0,)))

        @pl.when(m == micro - 1)
        def _():
            state[...] = ssm_t[...].T.reshape(state.shape)

        def take(t):
            remote(
                sum_send.at[t], sum_recv.at[m, t], sum_s, sum_r.at[m, t], sibling
            ).wait_recv()
            total[...] += sum_recv[m, t].astype(F32)

        each(1, n_chip, take)
        passed[m] = total[...].astype(BF16)

        @pl.when(z < n_pipe - 1)
        def _():
            remote(passed.at[m], h_all.at[m, me], pass_s, pass_r.at[m], me, z + 1).start()

        for i in range(n_head):
            out_send[m, i] = total[pl.ds(i * rows, rows), :].astype(BF16)

        def give_out(t):
            to = lax.rem(me + t, n_head)
            remote(
                out_send.at[m, to],
                out.at[m, :, pl.ds(pl.multiple_of(me * chunk, chunk), chunk)],
                out_s,
                out_r.at[m],
                to,
            ).start()

        each(1, n_head, give_out)
        pltpu.make_async_copy(
            out_send.at[m, me],
            out.at[m, :, pl.ds(pl.multiple_of(me * chunk, chunk), chunk)],
            own_s,
        ).start()

        drain(out_send.at[m, 0], own_s)
        drain(h_all.at[m, pl.ds(0, n_head - 1)], ag_s)
        drain(bc_recv.at[m, pl.ds(0, n_head - 1)], bc_s)
        drain(sib_send, sib_s)
        drain(sum_send.at[pl.ds(1, n_chip - 1)], sum_s)
        drain(out_send.at[m, pl.ds(0, n_head - 1)], out_s)

        @pl.when(z < n_pipe - 1)
        def _():
            remote(passed.at[m], h_all.at[m, me], pass_s, pass_r.at[m], me).wait_send()

        @pl.when(z == 0)
        def _():
            drain(first_in.at[m, pl.ds(0, n_head - 1)], first_s.at[m])

    each(0, micro, block)
    for m in range(micro):
        drain(out.at[m, :, pl.ds(0, (n_head - 1) * chunk)], out_r.at[m])


def per_device(
    sizes,
    hidden,
    norm_gain,
    w_x,
    w_bc,
    w_dt,
    conv_x,
    conv_bc,
    dt_bias,
    a_rate,
    d_skip,
    w_out,
    ssm_init,
    conv_x_init,
    conv_bc_init,
):
    n_pipe, n_head, n_x, n_y = sizes
    n_chip = n_head // 2
    micro, rows, width = hidden.shape
    tokens = rows * n_head
    chunk = width // n_head
    inner = w_x.shape[2]
    heads = dt_bias.shape[1]
    bc_cols = w_bc.shape[2]
    group = lax.axis_index("head") // (n_head // GROUPS)

    def own_group(values):
        split = values[0].reshape(values.shape[1], -1, GROUPS)
        return lax.dynamic_index_in_dim(split, group, 2, keepdims=False)

    taps = jnp.concatenate([conv_x[0], own_group(conv_bc)], axis=1)
    tails = jnp.concatenate([conv_x_init[0], own_group(conv_bc_init)], axis=1)
    vmem = pl.BlockSpec(memory_space=pltpu.VMEM)
    far = pl.BlockSpec(memory_space=pl.ANY)
    dma = pltpu.SemaphoreType.DMA
    out, state = pl.pallas_call(
        functools.partial(section, sizes),
        out_shape=(
            jax.ShapeDtypeStruct((micro, rows, width), BF16),
            jax.ShapeDtypeStruct(ssm_init.shape[1:], F32),
        ),
        in_specs=[vmem, vmem, far, far, far, far, far, vmem, vmem, vmem, vmem, vmem],
        out_specs=(vmem, vmem),
        scratch_shapes=[
            pltpu.VMEM((n_chip, 2 * chunk, inner), BF16),
            pltpu.VMEM((n_chip, 2 * chunk, 256), BF16),
            pltpu.VMEM((n_chip, 2 * chunk, heads), BF16),
            pltpu.VMEM((n_head, inner, chunk), BF16),
            pltpu.VMEM(ssm_init.shape[1:], F32),
            pltpu.VMEM((STATE, inner), F32),
            pltpu.VMEM((micro, n_head, tokens, chunk), BF16),
            pltpu.VMEM((micro, n_head, rows, chunk), BF16),
            pltpu.VMEM((tokens, inner + 256), F32),
            pltpu.VMEM((tokens, 128), F32),
            pltpu.VMEM((8 + tokens, inner + 2 * STATE), F32),
            pltpu.VMEM((GROUPS, bc_cols // GROUPS, 128), BF16),
            pltpu.VMEM((micro, n_head, bc_cols // GROUPS, 128), BF16),
            pltpu.VMEM((tokens, inner), BF16),
            pltpu.VMEM((tokens, inner), BF16),
            pltpu.VMEM((tokens, STATE), BF16),
            pltpu.VMEM((8, inner), F32),
            pltpu.VMEM((n_chip, tokens, chunk), BF16),
            pltpu.VMEM((micro, n_chip, tokens, chunk), BF16),
            pltpu.VMEM((n_chip, tokens, chunk), BF16),
            pltpu.VMEM((micro, n_chip, tokens, chunk), BF16),
            pltpu.VMEM((tokens, chunk), F32),
            pltpu.VMEM((micro, tokens, chunk), BF16),
            pltpu.VMEM((micro, n_head, rows, chunk), BF16),
            dma((5,)),
            dma((micro,)),
            dma((micro,)),
            dma,
            dma((micro, n_chip)),
            dma((micro, n_chip)),
            dma,
            dma((micro,)),
            dma,
            dma((micro, n_chip)),
            dma,
            dma((micro, n_chip)),
            dma,
            dma((micro,)),
            dma,
            dma((micro,)),
            dma,
        ],
        compiler_params=pltpu.CompilerParams(
            collective_id=0, has_side_effects=True, vmem_limit_bytes=48 << 20
        ),
    )(
        hidden,
        norm_gain.reshape(n_chip, 1, 2 * chunk),
        w_x.reshape(n_chip, 2 * chunk, inner),
        w_bc.reshape(n_chip, 2 * chunk, bc_cols),
        w_dt.reshape(n_chip, 2 * chunk, heads),
        w_out[0],
        ssm_init[0],
        taps,
        tails,
        dt_bias,
        a_rate,
        d_skip,
    )
    return (out[None], state[None])


def solution(mesh):
    n_pipe = mesh.shape["pipe"]
    n_head = mesh.shape["head"]
    n_x = 1
    while n_x * n_x < n_head // 2:
        n_x *= 2
    in_specs = (
        P(None, "head", None),
        P("pipe", None),
        P("pipe", None, "head"),
        P("pipe", None, "head"),
        P("pipe", None, "head"),
        P("pipe", None, "head"),
        P("pipe", None, None),
        P("pipe", "head"),
        P("pipe", "head"),
        P("pipe", "head"),
        P("pipe", "head", None),
        P("pipe", "head", None, None),
        P("pipe", None, "head"),
        P("pipe", None, None),
    )
    out_specs = (P("pipe", None, "head", None), P("pipe", "head", None, None))
    return jax.shard_map(
        functools.partial(per_device, (n_pipe, n_head, n_x, n_head // 2 // n_x)),
        mesh=mesh,
        in_specs=in_specs,
        out_specs=out_specs,
        check_vma=False,
    )
```

```python
import functools

import jax
import jax.numpy as jnp
from jax import lax
from jax.experimental import pallas as pl
from jax.experimental.pallas import tpu as pltpu
from jax.sharding import PartitionSpec as P

GROUPS = 8
STATE = 256
HEAD_DIM = 64
MESH = pl.DeviceIdType.MESH
F32 = jnp.float32
BF16 = jnp.bfloat16
AHEAD = 3
BEFORE = 6
LEAD = 4
STRIDE = 7


def dot(a, b, dims=((1,), (0,)), precision=None):
    return lax.dot_general(a, b, (dims, ((), ())), precision=precision, preferred_element_type=F32)


def exact(a, b):
    return dot(a, b, precision=lax.Precision.HIGHEST)


def section(
    sizes,
    hid,
    w_x,
    w_bc,
    w_dt,
    w_out,
    ssm_in,
    conv_x_in,
    conv_bc_in,
    tail_x_in,
    tail_bc_in,
    dt_bias_in,
    a_rate_in,
    d_skip_in,
    gain_in,
    out,
    state,
    gain,
    dt_bias,
    a_rate,
    d_skip,
    conv_x,
    conv_bc,
    tail_x,
    tail_bc,
    bc_rows,
    taps,
    scaled_v,
    wx_v,
    wbd_v,
    wdt_v,
    wo_v,
    ssm_v,
    ssm_t,
    h_all,
    first_in,
    acc,
    squares,
    padded,
    bc_send,
    bc_recv,
    y_v,
    x_end,
    b_end,
    decay_end,
    sib_send,
    sib_recv,
    sum_send,
    sum_recv,
    total,
    passed,
    out_send,
    load_sem,
    first_s,
    first_r,
    ag_s,
    ag_r,
    fwd_r,
    bc_s,
    bc_r,
    sib_s,
    sib_r,
    sum_s,
    sum_r,
    pass_s,
    pass_r,
    out_s,
    out_r,
    own_s,
    first_o,
):
    n_pipe, n_head, n_x, n_y = sizes
    n_chip = n_head // 2
    micro = hid.shape[0]
    rows = hid.shape[1]
    width = hid.shape[2]
    tokens = rows * n_head
    chunk = width // n_head
    inner = w_x.shape[2]
    heads = dt_bias.shape[1]
    bc_cols = w_bc.shape[2]
    per_group = n_head // GROUPS
    z = lax.axis_index("pipe")
    me = lax.axis_index("head")
    core = lax.rem(me, 2)
    chip = lax.div(me, 2)
    chip_x = lax.rem(chip, n_x)
    chip_y = lax.div(chip, n_x)
    sibling = chip * 2 + 1 - core

    def ahead(t):
        t = lax.rem(t * STRIDE, n_chip)
        return lax.rem(chip_y + lax.div(t, n_x), n_y) * n_x + lax.rem(chip_x + lax.rem(t, n_x), n_x)

    def behind(t):
        t = lax.rem(t * STRIDE, n_chip)
        return lax.rem(chip_y + n_y - lax.div(t, n_x), n_y) * n_x + lax.rem(
            chip_x + n_x - lax.rem(t, n_x), n_x
        )

    def remote(src, dst, send, recv, head, pipe=None):
        return pltpu.make_async_remote_copy(
            src_ref=src,
            dst_ref=dst,
            send_sem=send,
            recv_sem=recv,
            device_id={"pipe": z if pipe is None else pipe, "head": head},
            device_id_type=MESH,
        )

    def drain(ref, sem):
        pltpu.make_async_copy(ref, ref, sem).wait()

    def each(first, last, body):
        def step(t, carry):
            body(t)
            return carry

        lax.fori_loop(first, last, step, 0)

    small = (
        (gain_in, gain),
        (dt_bias_in, dt_bias),
        (a_rate_in, a_rate),
        (d_skip_in, d_skip),
        (conv_x_in, conv_x),
        (conv_bc_in, conv_bc),
        (tail_x_in, tail_x),
        (tail_bc_in, tail_bc),
        (w_dt, wdt_v),
        (ssm_in, ssm_v),
    )
    for k, (src, dst) in enumerate(small):
        pltpu.make_async_copy(src, dst, load_sem.at[3 + k]).start()

    barrier = pltpu.get_barrier_semaphore()

    def greet(t):
        pl.semaphore_signal(
            barrier,
            inc=1,
            device_id={"pipe": z, "head": lax.rem(me + t, n_head)},
            device_id_type=MESH,
        )

    each(1, n_head, greet)
    for other in (lax.rem(z + 1, n_pipe), lax.rem(z + n_pipe - 1, n_pipe)):
        pl.semaphore_signal(
            barrier, inc=1, device_id={"pipe": other, "head": me}, device_id_type=MESH
        )
    def load_in(k):
        pltpu.make_async_copy(w_x.at[k], wx_v.at[k], load_sem.at[0]).start()
        pltpu.make_async_copy(w_bc.at[k], wbd_v.at[k, :, pl.ds(0, bc_cols)], load_sem.at[1]).start()

    each(0, n_chip, load_in)

    for k, (src, dst) in enumerate(small):
        drain(dst, load_sem.at[3 + k])

    bc_all = conv_bc.shape[1]
    wide_k = 128 * GROUPS
    spans = bc_all // wide_k
    bc_rows[...] = jnp.zeros_like(bc_rows)
    bc_rows[0:4, :] = conv_bc[...]
    for k in range(3):
        bc_rows[4 + k : 5 + k, :] = tail_bc[k]
    pick_row = lax.broadcasted_iota(jnp.int32, (wide_k, 128), 0)
    pick_col = lax.broadcasted_iota(jnp.int32, (wide_k, 128), 1)
    pick = jnp.where(pick_row == pick_col * GROUPS + lax.div(me, per_group), 1.0, 0.0)
    spread_rows = jnp.concatenate(
        [bc_rows[:, k * wide_k : (k + 1) * wide_k] for k in range(spans)], axis=0
    )
    picked = exact(spread_rows, pick)
    taps[0:4, 0:inner] = conv_x[...]
    for k in range(3):
        taps[4 + k : 5 + k, 0:inner] = tail_x[k]
    for k in range(spans):
        taps[:, inner + k * 128 : inner + (k + 1) * 128] = picked[k * 8 : (k + 1) * 8]
    padded[5:8, :] = taps[4:7, :]

    dt_f = wdt_v[...].astype(F32)
    dt_cols = (
        jnp.concatenate([dt_f[:, k * 2 * chunk : (k + 1) * 2 * chunk] for k in range(n_chip)], axis=0)
        .T.astype(BF16)
        .astype(F32)
    )
    dt_at = lax.div(lax.broadcasted_iota(jnp.int32, dt_cols.shape, 1), heads)

    def join(k):
        wbd_v[k, :, bc_cols : bc_cols + 128] = jnp.where(dt_at == k, dt_cols, 0.0).astype(BF16)

    each(0, n_chip, join)
    ssm_t[...] = ssm_v[...].reshape(heads * HEAD_DIM, STATE).T
    pl.semaphore_wait(barrier, n_head + 1)

    def turn(m):
        def give(t):
            to = lax.rem(me + t, n_head)
            remote(
                hid.at[m, :, pl.ds(pl.multiple_of(to * chunk, chunk), chunk)],
                first_in.at[m, me],
                first_s.at[m],
                first_r.at[m],
                to,
            ).start()

        each(1, n_head, give)
        pltpu.make_async_copy(
            hid.at[m, :, pl.ds(pl.multiple_of(me * chunk, chunk), chunk)],
            first_in.at[m, me],
            first_o.at[m],
        ).start()

    def spread(m):
        mine = h_all.at[m, me]

        def give(t):
            remote(mine, mine, ag_s.at[m], ag_r.at[m, t], ahead(t) * 2 + core).start()

        each(1, n_chip, give)
        remote(mine, mine, ag_s.at[m], fwd_r.at[m, 0], sibling).start()

    def begin(m):
        drain(first_in.at[m, 0], first_o.at[m])
        drain(first_in.at[m, pl.ds(0, n_head - 1)], first_r.at[m])
        for i in range(n_head):
            total[pl.ds(i * rows, rows), :] = first_in[m, i].astype(F32)
        h_all[m, me] = total[...].astype(BF16)
        spread(m)

    @pl.when(z == 0)
    def _():
        turn(0)
        begin(0)
        for m in range(1, micro):
            turn(m)

    for k in range(n_head):
        pltpu.make_async_copy(
            w_out.at[:, pl.ds(k * chunk, chunk)], wo_v.at[k], load_sem.at[2]
        ).start()
    drain(wx_v, load_sem.at[0])
    drain(wbd_v.at[:, :, pl.ds(0, bc_cols)], load_sem.at[1])

    def carry_on(m):
        remote(passed.at[m], h_all.at[m, me], pass_s, pass_r.at[m], me).wait_recv()
        spread(m)

    @pl.when(z > 0)
    def _():
        carry_on(0)

    def block(m):
        more = m < micro - 1

        acc[...] = jnp.zeros_like(acc)
        squares[...] = jnp.zeros_like(squares)

        def relay(t):
            got = h_all.at[m, behind(t) * 2 + core]
            copy = remote(got, got, ag_s.at[m], ag_r.at[m, t], sibling)
            copy.wait_recv()
            remote(got, got, ag_s.at[m], fwd_r.at[m, t], sibling).start()

        each(1, 1 + AHEAD, relay)

        def project(t):
            @pl.when(t + 1 + AHEAD < n_chip)
            def _():
                relay(t + 1 + AHEAD)

            src = behind(t)
            theirs = h_all.at[m, src * 2 + 1 - core]
            remote(theirs, theirs, ag_s.at[m], fwd_r.at[m, t], sibling).wait_recv()
            values = jnp.concatenate([h_all[m, src * 2], h_all[m, src * 2 + 1]], axis=1).astype(F32)
            sq = values * values
            part = sq[:, 0:128]
            for k in range(1, 2 * chunk // 128):
                part = part + sq[:, k * 128 : (k + 1) * 128]
            squares[...] += part
            scaled = (values * gain[src]).astype(BF16)
            acc[:, inner : inner + 256] += dot(scaled, wbd_v[src])
            return scaled

        def project_both(t):
            acc[:, 0:inner] += dot(project(t), wx_v[behind(t)])

        def project_later(t):
            scaled_v[t] = project(t)

        each(0, BEFORE, project_both)
        each(BEFORE, n_chip, project_later)
        inv = lax.rsqrt(jnp.sum(squares[...], axis=1, keepdims=True) / width + 1e-05)

        bc_dt = acc[:, inner : inner + 256] * inv
        bc_bf = bc_dt[:, 0:bc_cols].astype(BF16)
        bc_wide = jnp.concatenate([bc_bf, jnp.zeros((128 - tokens, bc_cols), BF16)], axis=0)
        at_row = lax.broadcasted_iota(jnp.int32, (bc_cols, bc_cols), 0)
        at_col = lax.broadcasted_iota(jnp.int32, (bc_cols, bc_cols), 1)
        width_n = bc_cols // GROUPS
        wanted = lax.rem(at_row, width_n) * GROUPS + lax.div(at_row, width_n)
        order = jnp.where(at_col == wanted, 1.0, 0.0).astype(BF16)
        bc_send[...] = dot(order, bc_wide, ((1,), (1,))).astype(BF16).reshape(bc_send.shape)

        def give_bc(t):
            to = lax.rem(me + t, n_head)
            remote(
                bc_send.at[lax.div(to, per_group)], bc_recv.at[m, me], bc_s, bc_r.at[m], to
            ).start()

        each(1, n_head, give_bc)
        bc_recv[m, me] = bc_send[lax.div(me, per_group)]

        @pl.when(jnp.logical_and(z == 0, more))
        def _():
            begin(m + 1)


        def finish(t):
            acc[:, 0:inner] += dot(scaled_v[t], wx_v[behind(t)])

        each(BEFORE, n_chip, finish)
        padded[8 : 8 + tokens, 0:inner] = acc[:, 0:inner] * inv

        def conv(lo, hi):
            summed = taps[0:1, lo:hi] * padded[5 : 5 + tokens, lo:hi]
            for k in range(1, 4):
                summed = summed + taps[k : k + 1, lo:hi] * padded[5 + k : 5 + k + tokens, lo:hi]
            return summed * lax.logistic(summed)

        x = conv(0, inner)
        fold_row = lax.broadcasted_iota(jnp.int32, (128, heads), 0)
        fold_col = lax.broadcasted_iota(jnp.int32, (128, heads), 1)
        fold = jnp.where(lax.rem(fold_row, heads) == fold_col, 1.0, 0.0)
        raw = exact(bc_dt[:, bc_cols : bc_cols + 128], fold) + dt_bias[...]
        step = jnp.maximum(raw, 0.0) + jnp.log1p(jnp.exp(-jnp.abs(raw)))
        tri_row = lax.broadcasted_iota(jnp.int32, (tokens, tokens), 0)
        tri_col = lax.broadcasted_iota(jnp.int32, (tokens, tokens), 1)
        log_decay = exact(jnp.where(tri_row >= tri_col, 1.0, 0.0), -step * a_rate[...])
        head_row = lax.broadcasted_iota(jnp.int32, (heads, inner), 0)
        head_col = lax.div(lax.broadcasted_iota(jnp.int32, (heads, inner), 1), HEAD_DIM)
        of_head = jnp.where(head_row == head_col, 1.0, 0.0)
        skip8 = jnp.broadcast_to(d_skip[...], (8, heads))
        wide = exact(jnp.concatenate([step, log_decay, skip8], axis=0), of_head)
        step_w = wide[0:tokens]
        log_w = wide[tokens : 2 * tokens]
        skip_w = wide[2 * tokens : 2 * tokens + 1]
        at_t = lax.broadcasted_iota(jnp.int32, (tokens, inner), 0)
        at_s = lax.rem(lax.broadcasted_iota(jnp.int32, (tokens, inner), 1), HEAD_DIM)
        log_s = jnp.sum(jnp.where(at_t == at_s, log_w, 0.0), axis=0, keepdims=True)
        causal = at_t >= at_s
        pair = jnp.where(causal, jnp.exp(jnp.where(causal, log_w - log_s, 0.0)), 0.0)
        log_end = log_w[tokens - 1 : tokens]
        x_dt = x * step_w
        x_end[...] = (jnp.exp(log_end - log_w) * x_dt).astype(BF16)
        decay_end[0:1, :] = jnp.exp(log_end)

        drain(bc_recv.at[m, pl.ds(0, n_head - 1)], bc_r.at[m])
        both = bc_recv[m].reshape(2 * STATE, 128).astype(F32).T
        padded[8 : 8 + tokens, inner : inner + 2 * STATE] = both[0:tokens]
        bc = conv(inner, inner + 2 * STATE)
        padded[5:8, :] = padded[5 + tokens : 8 + tokens, :]
        b_v = bc[:, 0:STATE].astype(BF16)
        c_v = bc[:, STATE : 2 * STATE].astype(BF16)
        b_end[...] = b_v
        scores = dot(c_v, jnp.concatenate([b_v, b_v], axis=0), ((1,), (1,)))
        weight = (jnp.concatenate([scores] * (heads // 2), axis=1) * pair).astype(BF16)
        lane = lax.broadcasted_iota(jnp.int32, (tokens, 2 * HEAD_DIM), 1)
        within = []
        for k in range(heads // 2):
            cols = slice(k * 2 * HEAD_DIM, (k + 1) * 2 * HEAD_DIM)
            two = x_dt[:, cols]
            stacked = jnp.concatenate(
                [jnp.where(lane < HEAD_DIM, two, 0.0), jnp.where(lane < HEAD_DIM, 0.0, two)], axis=0
            ).astype(BF16)
            within.append(dot(weight[:, cols], stacked))
        carried = jnp.exp(log_w) * dot(c_v, ssm_t[...].astype(BF16))
        y_v[...] = (jnp.concatenate(within, axis=1) + carried + skip_w * x).astype(BF16)

        @pl.when(m == 0)
        def _():
            drain(wo_v, load_sem.at[2])

        def for_sibling(i):
            t = lax.rem(i + 1, n_chip)
            sib_send[t] = dot(y_v[...], wo_v[ahead(t) * 2 + 1 - core]).astype(BF16)
            remote(sib_send.at[t], sib_recv.at[m, t], sib_s, sib_r.at[m, t], sibling).start()

        def product(t):
            return dot(y_v[...], wo_v[ahead(t) * 2 + core]).astype(BF16).astype(F32)

        def chip_sum(t, part):
            remote(
                sib_send.at[t], sib_recv.at[m, t], sib_s, sib_r.at[m, t], sibling
            ).wait_recv()
            return part + sib_recv[m, t].astype(F32)

        def for_owner(t, part):
            sum_send[t] = chip_sum(t, part).astype(BF16)
            remote(
                sum_send.at[t],
                sum_recv.at[m, t],
                sum_s,
                sum_r.at[m, t],
                ahead(t) * 2 + core,
            ).start()

        def for_both(i):
            part = product(i + 1)
            for_sibling(i + LEAD)
            for_owner(i + 1, part)

        each(0, LEAD, for_sibling)
        each(0, n_chip - LEAD, for_both)
        for t in range(n_chip - LEAD + 1, n_chip):
            for_owner(t, product(t))
        total[...] = chip_sum(0, product(0)) + h_all[m, me].astype(F32)

        ssm_t[...] = decay_end[0:1, :] * ssm_t[...] + dot(b_end[...], x_end[...], ((0,), (0,)))

        @pl.when(m == micro - 1)
        def _():
            state[...] = ssm_t[...].T.reshape(state.shape)

        def take(t):
            remote(
                sum_send.at[t], sum_recv.at[m, t], sum_s, sum_r.at[m, t], sibling
            ).wait_recv()
            total[...] += sum_recv[m, t].astype(F32)

        each(1, n_chip, take)
        passed[m] = total[...].astype(BF16)

        @pl.when(z < n_pipe - 1)
        def _():
            remote(passed.at[m], h_all.at[m, me], pass_s, pass_r.at[m], me, z + 1).start()

        @pl.when(jnp.logical_and(z > 0, more))
        def _():
            carry_on(m + 1)

        for i in range(n_head):
            out_send[m, i] = total[pl.ds(i * rows, rows), :].astype(BF16)

        def give_out(t):
            to = lax.rem(me + t, n_head)
            remote(
                out_send.at[m, to],
                out.at[m, :, pl.ds(pl.multiple_of(me * chunk, chunk), chunk)],
                out_s,
                out_r.at[m],
                to,
            ).start()

        each(1, n_head, give_out)
        pltpu.make_async_copy(
            out_send.at[m, me],
            out.at[m, :, pl.ds(pl.multiple_of(me * chunk, chunk), chunk)],
            own_s,
        ).start()

        drain(out_send.at[m, 0], own_s)
        drain(h_all.at[m, pl.ds(0, n_head - 1)], ag_s.at[m])
        drain(bc_recv.at[m, pl.ds(0, n_head - 1)], bc_s)
        drain(sib_send, sib_s)
        drain(sum_send.at[pl.ds(1, n_chip - 1)], sum_s)
        drain(out_send.at[m, pl.ds(0, n_head - 1)], out_s)

        @pl.when(z < n_pipe - 1)
        def _():
            remote(passed.at[m], h_all.at[m, me], pass_s, pass_r.at[m], me).wait_send()

        @pl.when(z == 0)
        def _():
            drain(first_in.at[m, pl.ds(0, n_head - 1)], first_s.at[m])

    each(0, micro, block)
    for m in range(micro):
        drain(out.at[m, :, pl.ds(0, (n_head - 1) * chunk)], out_r.at[m])


def per_device(
    sizes,
    hidden,
    norm_gain,
    w_x,
    w_bc,
    w_dt,
    conv_x,
    conv_bc,
    dt_bias,
    a_rate,
    d_skip,
    w_out,
    ssm_init,
    conv_x_init,
    conv_bc_init,
):
    n_pipe, n_head, n_x, n_y = sizes
    n_chip = n_head // 2
    micro, rows, width = hidden.shape
    tokens = rows * n_head
    chunk = width // n_head
    inner = w_x.shape[2]
    heads = dt_bias.shape[1]
    bc_cols = w_bc.shape[2]
    vmem = pl.BlockSpec(memory_space=pltpu.VMEM)
    far = pl.BlockSpec(memory_space=pltpu.HBM)
    dma = pltpu.SemaphoreType.DMA
    out, state = pl.pallas_call(
        functools.partial(section, sizes),
        out_shape=(
            jax.ShapeDtypeStruct((micro, rows, width), BF16),
            jax.ShapeDtypeStruct(ssm_init.shape[1:], F32),
        ),
        in_specs=[far] * 14,
        out_specs=(vmem, vmem),
        scratch_shapes=[
            pltpu.VMEM((n_chip, 1, 2 * chunk), F32),
            pltpu.VMEM((1, heads), F32),
            pltpu.VMEM((1, heads), F32),
            pltpu.VMEM((1, heads), F32),
            pltpu.VMEM(conv_x.shape[1:], F32),
            pltpu.VMEM(conv_bc.shape[1:], F32),
            pltpu.VMEM((conv_x_init.shape[1], 1, conv_x_init.shape[2]), F32),
            pltpu.VMEM((conv_bc_init.shape[1], 1, conv_bc_init.shape[2]), F32),
            pltpu.VMEM((8, conv_bc.shape[2]), F32),
            pltpu.VMEM((8, inner + 2 * STATE), F32),
            pltpu.VMEM((n_chip, tokens, 2 * chunk), BF16),
            pltpu.VMEM((n_chip, 2 * chunk, inner), BF16),
            pltpu.VMEM((n_chip, 2 * chunk, 256), BF16),
            pltpu.VMEM((heads, width), BF16),
            pltpu.VMEM((n_head, inner, chunk), BF16),
            pltpu.VMEM(ssm_init.shape[1:], F32),
            pltpu.VMEM((STATE, inner), F32),
            pltpu.VMEM((micro, n_head, tokens, chunk), BF16),
            pltpu.VMEM((micro, n_head, rows, chunk), BF16),
            pltpu.VMEM((tokens, inner + 256), F32),
            pltpu.VMEM((tokens, 128), F32),
            pltpu.VMEM((8 + tokens, inner + 2 * STATE), F32),
            pltpu.VMEM((GROUPS, bc_cols // GROUPS, 128), BF16),
            pltpu.VMEM((micro, n_head, bc_cols // GROUPS, 128), BF16),
            pltpu.VMEM((tokens, inner), BF16),
            pltpu.VMEM((tokens, inner), BF16),
            pltpu.VMEM((tokens, STATE), BF16),
            pltpu.VMEM((8, inner), F32),
            pltpu.VMEM((n_chip, tokens, chunk), BF16),
            pltpu.VMEM((micro, n_chip, tokens, chunk), BF16),
            pltpu.VMEM((n_chip, tokens, chunk), BF16),
            pltpu.VMEM((micro, n_chip, tokens, chunk), BF16),
            pltpu.VMEM((tokens, chunk), F32),
            pltpu.VMEM((micro, tokens, chunk), BF16),
            pltpu.VMEM((micro, n_head, rows, chunk), BF16),
            dma((13,)),
            dma((micro,)),
            dma((micro,)),
            dma((micro,)),
            dma((micro, n_chip)),
            dma((micro, n_chip)),
            dma,
            dma((micro,)),
            dma,
            dma((micro, n_chip)),
            dma,
            dma((micro, n_chip)),
            dma,
            dma((micro,)),
            dma,
            dma((micro,)),
            dma,
            dma((micro,)),
        ],
        compiler_params=pltpu.CompilerParams(
            collective_id=0, has_side_effects=True, vmem_limit_bytes=48 << 20
        ),
    )(
        *(
            pltpu.with_memory_space_constraint(value, pltpu.HBM)
            for value in (
                hidden,
                w_x.reshape(n_chip, 2 * chunk, inner),
                w_bc.reshape(n_chip, 2 * chunk, bc_cols),
                w_dt[0].T,
                w_out[0],
                ssm_init[0],
                conv_x[0],
                conv_bc[0],
                conv_x_init.transpose(1, 0, 2),
                conv_bc_init.transpose(1, 0, 2),
                dt_bias,
                a_rate,
                d_skip,
                norm_gain.reshape(n_chip, 1, 2 * chunk),
            )
        )
    )
    return (out[None], state[None])


def solution(mesh):
    n_pipe = mesh.shape["pipe"]
    n_head = mesh.shape["head"]
    n_x = 1
    while n_x * n_x < n_head // 2:
        n_x *= 2
    in_specs = (
        P(None, "head", None),
        P("pipe", None),
        P("pipe", None, "head"),
        P("pipe", None, "head"),
        P("pipe", None, "head"),
        P("pipe", None, "head"),
        P("pipe", None, None),
        P("pipe", "head"),
        P("pipe", "head"),
        P("pipe", "head"),
        P("pipe", "head", None),
        P("pipe", "head", None, None),
        P("pipe", None, "head"),
        P("pipe", None, None),
    )
    out_specs = (P("pipe", None, "head", None), P("pipe", "head", None, None))
    return jax.shard_map(
        functools.partial(per_device, (n_pipe, n_head, n_x, n_head // 2 // n_x)),
        mesh=mesh,
        in_specs=in_specs,
        out_specs=out_specs,
        check_vma=False,
    )
```

```python
import functools

import jax
import jax.numpy as jnp
from jax import lax
from jax.experimental import pallas as pl
from jax.experimental.pallas import tpu as pltpu
from jax.sharding import PartitionSpec as P

GROUPS = 8
STATE = 256
HEAD_DIM = 64
MESH = pl.DeviceIdType.MESH
F32 = jnp.float32
BF16 = jnp.bfloat16
AHEAD = 4
EARLY = 7
BEFORE = 6
LEAD = 4
SIDE = 4
NEAR = (2, 8, 1, 4, 3, 12, 5, 7, 13, 15)
ORDER = (0, 1, 4, 3, 12, 2, 8, 5, 7, 13, 15, 6, 14, 9, 11, 10)
HANDED = {2: (4, 12, 8), 8: (1, 3)}


def dot(a, b, dims=((1,), (0,)), precision=None):
    return lax.dot_general(a, b, (dims, ((), ())), precision=precision, preferred_element_type=F32)


def exact(a, b):
    return dot(a, b, precision=lax.Precision.HIGHEST)


def section(
    sizes,
    hid,
    w_x,
    w_bc,
    w_dt,
    w_out,
    ssm_in,
    conv_x_in,
    conv_bc_in,
    tail_x_in,
    tail_bc_in,
    dt_bias_in,
    a_rate_in,
    d_skip_in,
    gain_in,
    out,
    state,
    gain,
    dt_bias,
    a_rate,
    d_skip,
    conv_x,
    conv_bc,
    tail_x,
    tail_bc,
    bc_rows,
    taps,
    scaled_v,
    wx_v,
    wbd_v,
    wdt_v,
    wo_v,
    ssm_v,
    ssm_t,
    h_all,
    first_in,
    acc,
    squares,
    padded,
    bc_send,
    bc_recv,
    y_v,
    x_end,
    b_end,
    decay_end,
    sib_send,
    sib_recv,
    sum_send,
    sum_recv,
    total,
    passed,
    out_send,
    load_sem,
    first_s,
    first_r,
    ag_s,
    ag_r,
    fwd_r,
    bc_s,
    bc_r,
    sib_s,
    sib_r,
    sum_s,
    sum_r,
    pass_s,
    pass_r,
    out_s,
    out_r,
    own_s,
    first_o,
):
    n_pipe, n_head, n_x, n_y = sizes
    n_chip = n_head // 2
    micro = hid.shape[0]
    rows = hid.shape[1]
    width = hid.shape[2]
    tokens = rows * n_head
    chunk = width // n_head
    inner = w_x.shape[2]
    heads = dt_bias.shape[1]
    bc_cols = w_bc.shape[2]
    per_group = n_head // GROUPS
    z = lax.axis_index("pipe")
    me = lax.axis_index("head")
    core = lax.rem(me, 2)
    chip = lax.div(me, 2)
    chip_x = lax.rem(chip, n_x)
    chip_y = lax.div(chip, n_x)
    sibling = chip * 2 + 1 - core

    def ahead(t):
        return lax.rem(chip_y + lax.div(t, n_x), n_y) * n_x + lax.rem(chip_x + lax.rem(t, n_x), n_x)

    def behind(t):
        return lax.rem(chip_y + n_y - lax.div(t, n_x), n_y) * n_x + lax.rem(
            chip_x + n_x - lax.rem(t, n_x), n_x
        )

    def nearest(t):
        value = ORDER[0] + 0 * t
        for k in range(1, n_chip):
            value = value + (ORDER[k] - ORDER[k - 1]) * lax.div(t + n_chip - k, n_chip)
        return value

    def mixed(t):
        return ahead(nearest(lax.rem(n_chip - t, n_chip)))

    def remote(src, dst, send, recv, head, pipe=None):
        return pltpu.make_async_remote_copy(
            src_ref=src,
            dst_ref=dst,
            send_sem=send,
            recv_sem=recv,
            device_id={"pipe": z if pipe is None else pipe, "head": head},
            device_id_type=MESH,
        )

    def drain(ref, sem):
        pltpu.make_async_copy(ref, ref, sem).wait()

    def each(first, last, body):
        def step(t, carry):
            body(t)
            return carry

        lax.fori_loop(first, last, step, 0)

    small = (
        (gain_in, gain),
        (dt_bias_in, dt_bias),
        (a_rate_in, a_rate),
        (d_skip_in, d_skip),
        (conv_x_in, conv_x),
        (conv_bc_in, conv_bc),
        (tail_x_in, tail_x),
        (tail_bc_in, tail_bc),
        (w_dt, wdt_v),
        (ssm_in, ssm_v),
    )
    for k, (src, dst) in enumerate(small):
        pltpu.make_async_copy(src, dst, load_sem.at[3 + k]).start()

    barrier = pltpu.get_barrier_semaphore()

    def greet(t):
        pl.semaphore_signal(
            barrier,
            inc=1,
            device_id={"pipe": z, "head": lax.rem(me + t, n_head)},
            device_id_type=MESH,
        )

    each(1, n_head, greet)
    for other in (lax.rem(z + 1, n_pipe), lax.rem(z + n_pipe - 1, n_pipe)):
        pl.semaphore_signal(
            barrier, inc=1, device_id={"pipe": other, "head": me}, device_id_type=MESH
        )
    def load_in(k):
        pltpu.make_async_copy(w_x.at[k], wx_v.at[k], load_sem.at[0]).start()
        pltpu.make_async_copy(w_bc.at[k], wbd_v.at[k, :, pl.ds(0, bc_cols)], load_sem.at[1]).start()

    each(0, n_chip, load_in)

    for k, (src, dst) in enumerate(small):
        drain(dst, load_sem.at[3 + k])

    bc_all = conv_bc.shape[1]
    wide_k = 128 * GROUPS
    spans = bc_all // wide_k
    bc_rows[...] = jnp.zeros_like(bc_rows)
    bc_rows[0:4, :] = conv_bc[...]
    for k in range(3):
        bc_rows[4 + k : 5 + k, :] = tail_bc[k]
    pick_row = lax.broadcasted_iota(jnp.int32, (wide_k, 128), 0)
    pick_col = lax.broadcasted_iota(jnp.int32, (wide_k, 128), 1)
    pick = jnp.where(pick_row == pick_col * GROUPS + lax.div(me, per_group), 1.0, 0.0)
    spread_rows = jnp.concatenate(
        [bc_rows[:, k * wide_k : (k + 1) * wide_k] for k in range(spans)], axis=0
    )
    picked = exact(spread_rows, pick)
    taps[0:4, 0:inner] = conv_x[...]
    for k in range(3):
        taps[4 + k : 5 + k, 0:inner] = tail_x[k]
    for k in range(spans):
        taps[:, inner + k * 128 : inner + (k + 1) * 128] = picked[k * 8 : (k + 1) * 8]
    padded[5:8, :] = taps[4:7, :]

    dt_f = wdt_v[...].astype(F32)
    dt_cols = (
        jnp.concatenate([dt_f[:, k * 2 * chunk : (k + 1) * 2 * chunk] for k in range(n_chip)], axis=0)
        .T.astype(BF16)
        .astype(F32)
    )
    dt_at = lax.div(lax.broadcasted_iota(jnp.int32, dt_cols.shape, 1), heads)

    def join(k):
        wbd_v[k, :, bc_cols : bc_cols + 128] = jnp.where(dt_at == k, dt_cols, 0.0).astype(BF16)

    each(0, n_chip, join)
    ssm_t[...] = ssm_v[...].reshape(heads * HEAD_DIM, STATE).T
    pl.semaphore_wait(barrier, n_head + 1)

    def turn(m):
        def give(t):
            to = lax.rem(me + t, n_head)
            remote(
                hid.at[m, :, pl.ds(pl.multiple_of(to * chunk, chunk), chunk)],
                first_in.at[m, me],
                first_s.at[m],
                first_r.at[m],
                to,
            ).start()

        each(1, n_head, give)
        pltpu.make_async_copy(
            hid.at[m, :, pl.ds(pl.multiple_of(me * chunk, chunk), chunk)],
            first_in.at[m, me],
            first_o.at[m],
        ).start()

    def spread(m):
        mine = h_all.at[m, me]

        for u in NEAR:
            remote(mine, mine, ag_s.at[m], ag_r.at[m, u], ahead(u) * 2 + core).start()
        remote(mine, mine, ag_s.at[m], fwd_r.at[m, 0], sibling).start()

    def begin(m):
        drain(first_in.at[m, 0], first_o.at[m])
        drain(first_in.at[m, pl.ds(0, n_head - 1)], first_r.at[m])
        for i in range(n_head):
            total[pl.ds(i * rows, rows), :] = first_in[m, i].astype(F32)
        h_all[m, me] = total[...].astype(BF16)
        spread(m)

    @pl.when(z == 0)
    def _():
        turn(0)
        begin(0)
        for m in range(1, micro):
            turn(m)

    for k in range(n_head):
        pltpu.make_async_copy(
            w_out.at[:, pl.ds(k * chunk, chunk)], wo_v.at[k], load_sem.at[2]
        ).start()
    drain(wx_v, load_sem.at[0])
    drain(wbd_v.at[:, :, pl.ds(0, bc_cols)], load_sem.at[1])

    def carry_on(m):
        remote(passed.at[m], h_all.at[m, me], pass_s, pass_r.at[m], me).wait_recv()
        spread(m)

    @pl.when(z > 0)
    def _():
        carry_on(0)

    def block(m):
        more = m < micro - 1

        acc[...] = jnp.zeros_like(acc)
        squares[...] = jnp.zeros_like(squares)

        def relay(u, handed=()):
            got = h_all.at[m, behind(u) * 2 + core]
            copy = remote(got, got, ag_s.at[m], ag_r.at[m, u], sibling)
            copy.wait_recv()
            for v in handed:
                remote(got, got, ag_s.at[m], ag_r.at[m, u + v], ahead(v) * 2 + core).start()
            remote(got, got, ag_s.at[m], fwd_r.at[m, u], sibling).start()

        for u in ORDER[1:EARLY]:
            relay(u, HANDED.get(u, ()))

        def project(t):
            @pl.when(jnp.logical_and(t + AHEAD >= EARLY, t + AHEAD < n_chip))
            def _():
                relay(nearest(t + AHEAD))

            u = nearest(t)
            src = behind(u)
            theirs = h_all.at[m, src * 2 + 1 - core]
            remote(theirs, theirs, ag_s.at[m], fwd_r.at[m, u], sibling).wait_recv()
            values = jnp.concatenate([h_all[m, src * 2], h_all[m, src * 2 + 1]], axis=1).astype(F32)
            sq = values * values
            part = sq[:, 0:128]
            for k in range(1, 2 * chunk // 128):
                part = part + sq[:, k * 128 : (k + 1) * 128]
            squares[...] += part
            scaled = (values * gain[src]).astype(BF16)
            acc[:, inner : inner + 256] += dot(scaled, wbd_v[src])
            return scaled

        def project_both(t):
            acc[:, 0:inner] += dot(project(t), wx_v[behind(nearest(t))])

        def project_later(t):
            scaled_v[t] = project(t)

        each(0, BEFORE, project_both)
        each(BEFORE, n_chip, project_later)
        inv = lax.rsqrt(jnp.sum(squares[...], axis=1, keepdims=True) / width + 1e-05)

        bc_dt = acc[:, inner : inner + 256] * inv
        bc_bf = bc_dt[:, 0:bc_cols].astype(BF16)
        bc_wide = jnp.concatenate([bc_bf, jnp.zeros((128 - tokens, bc_cols), BF16)], axis=0)
        at_row = lax.broadcasted_iota(jnp.int32, (bc_cols, bc_cols), 0)
        at_col = lax.broadcasted_iota(jnp.int32, (bc_cols, bc_cols), 1)
        width_n = bc_cols // GROUPS
        wanted = lax.rem(at_row, width_n) * GROUPS + lax.div(at_row, width_n)
        order = jnp.where(at_col == wanted, 1.0, 0.0).astype(BF16)
        bc_send[m] = dot(order, bc_wide, ((1,), (1,))).astype(BF16).reshape(bc_send.shape[1:])

        def give_bc(t):
            to = lax.rem(me + t, n_head)
            remote(
                bc_send.at[m, lax.div(to, per_group)], bc_recv.at[m, me], bc_s, bc_r.at[m], to
            ).start()

        each(1, n_head, give_bc)
        bc_recv[m, me] = bc_send[m, lax.div(me, per_group)]

        @pl.when(jnp.logical_and(z == 0, more))
        def _():
            begin(m + 1)


        def finish(t):
            acc[:, 0:inner] += dot(scaled_v[t], wx_v[behind(nearest(t))])

        each(BEFORE, n_chip, finish)
        padded[8 : 8 + tokens, 0:inner] = acc[:, 0:inner] * inv

        def conv(lo, hi):
            summed = taps[0:1, lo:hi] * padded[5 : 5 + tokens, lo:hi]
            for k in range(1, 4):
                summed = summed + taps[k : k + 1, lo:hi] * padded[5 + k : 5 + k + tokens, lo:hi]
            return summed * lax.logistic(summed)

        x = conv(0, inner)
        fold_row = lax.broadcasted_iota(jnp.int32, (128, heads), 0)
        fold_col = lax.broadcasted_iota(jnp.int32, (128, heads), 1)
        fold = jnp.where(lax.rem(fold_row, heads) == fold_col, 1.0, 0.0)
        raw = exact(bc_dt[:, bc_cols : bc_cols + 128], fold) + dt_bias[...]
        step = jnp.maximum(raw, 0.0) + jnp.log1p(jnp.exp(-jnp.abs(raw)))
        tri_row = lax.broadcasted_iota(jnp.int32, (tokens, tokens), 0)
        tri_col = lax.broadcasted_iota(jnp.int32, (tokens, tokens), 1)
        log_decay = exact(jnp.where(tri_row >= tri_col, 1.0, 0.0), -step * a_rate[...])
        head_row = lax.broadcasted_iota(jnp.int32, (heads, inner), 0)
        head_col = lax.div(lax.broadcasted_iota(jnp.int32, (heads, inner), 1), HEAD_DIM)
        of_head = jnp.where(head_row == head_col, 1.0, 0.0)
        skip8 = jnp.broadcast_to(d_skip[...], (8, heads))
        wide = exact(jnp.concatenate([step, log_decay, skip8], axis=0), of_head)
        step_w = wide[0:tokens]
        log_w = wide[tokens : 2 * tokens]
        skip_w = wide[2 * tokens : 2 * tokens + 1]
        at_t = lax.broadcasted_iota(jnp.int32, (tokens, inner), 0)
        at_s = lax.rem(lax.broadcasted_iota(jnp.int32, (tokens, inner), 1), HEAD_DIM)
        log_s = jnp.sum(jnp.where(at_t == at_s, log_w, 0.0), axis=0, keepdims=True)
        causal = at_t >= at_s
        pair = jnp.where(causal, jnp.exp(jnp.where(causal, log_w - log_s, 0.0)), 0.0)
        log_end = log_w[tokens - 1 : tokens]
        x_dt = x * step_w
        x_end[...] = (jnp.exp(log_end - log_w) * x_dt).astype(BF16)
        decay_end[0:1, :] = jnp.exp(log_end)

        drain(bc_recv.at[m, pl.ds(0, n_head - 1)], bc_r.at[m])
        both = bc_recv[m].reshape(2 * STATE, 128).astype(F32).T
        padded[8 : 8 + tokens, inner : inner + 2 * STATE] = both[0:tokens]
        bc = conv(inner, inner + 2 * STATE)
        padded[5:8, :] = padded[5 + tokens : 8 + tokens, :]
        b_v = bc[:, 0:STATE].astype(BF16)
        c_v = bc[:, STATE : 2 * STATE].astype(BF16)
        b_end[...] = b_v
        scores = dot(c_v, jnp.concatenate([b_v, b_v], axis=0), ((1,), (1,)))
        weight = (jnp.concatenate([scores] * (heads // 2), axis=1) * pair).astype(BF16)
        lane = lax.broadcasted_iota(jnp.int32, (tokens, 2 * HEAD_DIM), 1)
        within = []
        for k in range(heads // 2):
            cols = slice(k * 2 * HEAD_DIM, (k + 1) * 2 * HEAD_DIM)
            two = x_dt[:, cols]
            stacked = jnp.concatenate(
                [jnp.where(lane < HEAD_DIM, two, 0.0), jnp.where(lane < HEAD_DIM, 0.0, two)], axis=0
            ).astype(BF16)
            within.append(dot(weight[:, cols], stacked))
        carried = jnp.exp(log_w) * dot(c_v, ssm_t[...].astype(BF16))
        y_v[...] = (jnp.concatenate(within, axis=1) + carried + skip_w * x).astype(BF16)

        @pl.when(m == 0)
        def _():
            drain(wo_v, load_sem.at[2])

        def for_sibling(i):
            t = lax.rem(i + 1, n_chip)
            sib_send[m, t] = dot(y_v[...], wo_v[mixed(t) * 2 + 1 - core]).astype(BF16)
            remote(sib_send.at[m, t], sib_recv.at[m, t], sib_s, sib_r.at[m, t], sibling).start()

        def product(t):
            return dot(y_v[...], wo_v[mixed(t) * 2 + core]).astype(BF16).astype(F32)

        def chip_sum(t, part):
            remote(
                sib_send.at[m, t], sib_recv.at[m, t], sib_s, sib_r.at[m, t], sibling
            ).wait_recv()
            return part + sib_recv[m, t].astype(F32)

        def for_owner(t, part):
            sum_send[m, t] = chip_sum(t, part).astype(BF16)
            remote(
                sum_send.at[m, t],
                sum_recv.at[m, t],
                sum_s,
                sum_r.at[m, t],
                mixed(t) * 2 + core,
            ).start()

        def for_both(i):
            part = product(i + 1)
            for_sibling(i + LEAD)
            for_owner(i + 1, part)

        each(0, LEAD, for_sibling)
        each(0, n_chip - LEAD, for_both)
        for t in range(n_chip - LEAD + 1, n_chip):
            for_owner(t, product(t))
        total[...] = chip_sum(0, product(0)) + h_all[m, me].astype(F32)

        ssm_t[...] = decay_end[0:1, :] * ssm_t[...] + dot(b_end[...], x_end[...], ((0,), (0,)))

        @pl.when(m == micro - 1)
        def _():
            state[...] = ssm_t[...].T.reshape(state.shape)

        def take(t):
            remote(
                sum_send.at[m, t], sum_recv.at[m, t], sum_s, sum_r.at[m, t], sibling
            ).wait_recv()
            total[...] += sum_recv[m, t].astype(F32)

        each(1, n_chip, take)
        passed[m] = total[...].astype(BF16)

        @pl.when(z < n_pipe - 1)
        def _():
            remote(passed.at[m], h_all.at[m, me], pass_s, pass_r.at[m], me, z + 1).start()

        @pl.when(jnp.logical_and(z > 0, more))
        def _():
            carry_on(m + 1)

        for i in range(n_head):
            out_send[m, i] = total[pl.ds(i * rows, rows), :].astype(BF16)

        def give_out(t):
            to = lax.rem(me + t, n_head)
            remote(
                out_send.at[m, to],
                out.at[m, :, pl.ds(pl.multiple_of(me * chunk, chunk), chunk)],
                out_s,
                out_r.at[m],
                to,
            ).start()

        each(1, n_head, give_out)
        pltpu.make_async_copy(
            out_send.at[m, me],
            out.at[m, :, pl.ds(pl.multiple_of(me * chunk, chunk), chunk)],
            own_s.at[m],
        ).start()

    each(0, micro, block)
    def settle(m):
        drain(out_send.at[m, 0], own_s.at[m])
        drain(h_all.at[m, pl.ds(0, n_head - 1)], ag_s.at[m])
        drain(bc_recv.at[m, pl.ds(0, n_head - 1)], bc_s)
        drain(sib_send.at[m], sib_s)
        drain(sum_send.at[m, pl.ds(1, n_chip - 1)], sum_s)
        drain(out_send.at[m, pl.ds(0, n_head - 1)], out_s)

        @pl.when(z < n_pipe - 1)
        def _():
            drain(passed.at[m], pass_s)

        @pl.when(z == 0)
        def _():
            drain(first_in.at[m, pl.ds(0, n_head - 1)], first_s.at[m])

        drain(out.at[m, :, pl.ds(0, (n_head - 1) * chunk)], out_r.at[m])

    each(0, micro, settle)


def per_device(
    sizes,
    hidden,
    norm_gain,
    w_x,
    w_bc,
    w_dt,
    conv_x,
    conv_bc,
    dt_bias,
    a_rate,
    d_skip,
    w_out,
    ssm_init,
    conv_x_init,
    conv_bc_init,
):
    n_pipe, n_head, n_x, n_y = sizes
    n_chip = n_head // 2
    micro, rows, width = hidden.shape
    tokens = rows * n_head
    chunk = width // n_head
    inner = w_x.shape[2]
    heads = dt_bias.shape[1]
    bc_cols = w_bc.shape[2]
    vmem = pl.BlockSpec(memory_space=pltpu.VMEM)
    far = pl.BlockSpec(memory_space=pltpu.HBM)
    dma = pltpu.SemaphoreType.DMA
    out, state = pl.pallas_call(
        functools.partial(section, sizes),
        out_shape=(
            jax.ShapeDtypeStruct((micro, rows, width), BF16),
            jax.ShapeDtypeStruct(ssm_init.shape[1:], F32),
        ),
        in_specs=[far] * 14,
        out_specs=(vmem, vmem),
        scratch_shapes=[
            pltpu.VMEM((n_chip, 1, 2 * chunk), F32),
            pltpu.VMEM((1, heads), F32),
            pltpu.VMEM((1, heads), F32),
            pltpu.VMEM((1, heads), F32),
            pltpu.VMEM(conv_x.shape[1:], F32),
            pltpu.VMEM(conv_bc.shape[1:], F32),
            pltpu.VMEM((conv_x_init.shape[1], 1, conv_x_init.shape[2]), F32),
            pltpu.VMEM((conv_bc_init.shape[1], 1, conv_bc_init.shape[2]), F32),
            pltpu.VMEM((8, conv_bc.shape[2]), F32),
            pltpu.VMEM((8, inner + 2 * STATE), F32),
            pltpu.VMEM((n_chip, tokens, 2 * chunk), BF16),
            pltpu.VMEM((n_chip, 2 * chunk, inner), BF16),
            pltpu.VMEM((n_chip, 2 * chunk, 256), BF16),
            pltpu.VMEM((heads, width), BF16),
            pltpu.VMEM((n_head, inner, chunk), BF16),
            pltpu.VMEM(ssm_init.shape[1:], F32),
            pltpu.VMEM((STATE, inner), F32),
            pltpu.VMEM((micro, n_head, tokens, chunk), BF16),
            pltpu.VMEM((micro, n_head, rows, chunk), BF16),
            pltpu.VMEM((tokens, inner + 256), F32),
            pltpu.VMEM((tokens, 128), F32),
            pltpu.VMEM((8 + tokens, inner + 2 * STATE), F32),
            pltpu.VMEM((micro, GROUPS, bc_cols // GROUPS, 128), BF16),
            pltpu.VMEM((micro, n_head, bc_cols // GROUPS, 128), BF16),
            pltpu.VMEM((tokens, inner), BF16),
            pltpu.VMEM((tokens, inner), BF16),
            pltpu.VMEM((tokens, STATE), BF16),
            pltpu.VMEM((8, inner), F32),
            pltpu.VMEM((micro, n_chip, tokens, chunk), BF16),
            pltpu.VMEM((micro, n_chip, tokens, chunk), BF16),
            pltpu.VMEM((micro, n_chip, tokens, chunk), BF16),
            pltpu.VMEM((micro, n_chip, tokens, chunk), BF16),
            pltpu.VMEM((tokens, chunk), F32),
            pltpu.VMEM((micro, tokens, chunk), BF16),
            pltpu.VMEM((micro, n_head, rows, chunk), BF16),
            dma((13,)),
            dma((micro,)),
            dma((micro,)),
            dma((micro,)),
            dma((micro, n_chip)),
            dma((micro, n_chip)),
            dma,
            dma((micro,)),
            dma,
            dma((micro, n_chip)),
            dma,
            dma((micro, n_chip)),
            dma,
            dma((micro,)),
            dma,
            dma((micro,)),
            dma((micro,)),
            dma((micro,)),
        ],
        compiler_params=pltpu.CompilerParams(
            collective_id=0, has_side_effects=True, vmem_limit_bytes=48 << 20
        ),
    )(
        *(
            pltpu.with_memory_space_constraint(value, pltpu.HBM)
            for value in (
                hidden,
                w_x.reshape(n_chip, 2 * chunk, inner),
                w_bc.reshape(n_chip, 2 * chunk, bc_cols),
                w_dt[0].T,
                w_out[0],
                ssm_init[0],
                conv_x[0],
                conv_bc[0],
                conv_x_init.transpose(1, 0, 2),
                conv_bc_init.transpose(1, 0, 2),
                dt_bias,
                a_rate,
                d_skip,
                norm_gain.reshape(n_chip, 1, 2 * chunk),
            )
        )
    )
    return (out[None], state[None])


def solution(mesh):
    n_pipe = mesh.shape["pipe"]
    n_head = mesh.shape["head"]
    n_x = SIDE
    in_specs = (
        P(None, "head", None),
        P("pipe", None),
        P("pipe", None, "head"),
        P("pipe", None, "head"),
        P("pipe", None, "head"),
        P("pipe", None, "head"),
        P("pipe", None, None),
        P("pipe", "head"),
        P("pipe", "head"),
        P("pipe", "head"),
        P("pipe", "head", None),
        P("pipe", "head", None, None),
        P("pipe", None, "head"),
        P("pipe", None, None),
    )
    out_specs = (P("pipe", None, "head", None), P("pipe", "head", None, None))
    return jax.shard_map(
        functools.partial(per_device, (n_pipe, n_head, n_x, n_head // 2 // n_x)),
        mesh=mesh,
        in_specs=in_specs,
        out_specs=out_specs,
        check_vma=False,
    )
```

```python
import functools

import jax
import jax.numpy as jnp
from jax import lax
from jax.experimental import pallas as pl
from jax.experimental.pallas import tpu as pltpu
from jax.sharding import PartitionSpec as P

GROUPS = 8
STATE = 256
HEAD_DIM = 64
MESH = pl.DeviceIdType.MESH
F32 = jnp.float32
BF16 = jnp.bfloat16
AHEAD = 4
EARLY = 7
BEFORE = 6
LEAD = 4
SIDE = 4
NEAR = (2, 8, 1, 4, 3, 12, 5, 7, 13, 15)
ORDER = (0, 2, 8, 1, 4, 3, 12, 5, 7, 13, 15, 6, 14, 9, 11, 10)
HANDED = {2: (4, 12, 8), 8: (1, 3)}


def dot(a, b, dims=((1,), (0,)), precision=None):
    return lax.dot_general(a, b, (dims, ((), ())), precision=precision, preferred_element_type=F32)


def exact(a, b):
    return dot(a, b, precision=lax.Precision.HIGHEST)


def section(
    sizes,
    hid,
    w_x,
    w_bc,
    w_dt,
    w_out,
    ssm_in,
    conv_x_in,
    conv_bc_in,
    tail_x_in,
    tail_bc_in,
    dt_bias_in,
    a_rate_in,
    d_skip_in,
    gain_in,
    out,
    state,
    gain,
    dt_bias,
    a_rate,
    d_skip,
    conv_x,
    conv_bc,
    tail_x,
    tail_bc,
    bc_rows,
    taps,
    scaled_v,
    wx_v,
    wbd_v,
    wdt_v,
    wo_v,
    ssm_v,
    ssm_t,
    h_all,
    first_in,
    acc,
    squares,
    padded,
    bc_send,
    bc_recv,
    y_v,
    x_end,
    b_end,
    decay_end,
    sib_send,
    sib_recv,
    sum_send,
    sum_recv,
    total,
    passed,
    out_send,
    load_sem,
    first_s,
    first_r,
    ag_s,
    ag_r,
    fwd_r,
    bc_s,
    bc_r,
    sib_s,
    sib_r,
    sum_s,
    sum_r,
    pass_s,
    pass_r,
    out_s,
    out_r,
    own_s,
    first_o,
):
    n_pipe, n_head, n_x, n_y = sizes
    n_chip = n_head // 2
    micro = hid.shape[0]
    rows = hid.shape[1]
    width = hid.shape[2]
    tokens = rows * n_head
    chunk = width // n_head
    inner = w_x.shape[2]
    heads = dt_bias.shape[1]
    bc_cols = w_bc.shape[2]
    per_group = n_head // GROUPS
    z = lax.axis_index("pipe")
    me = lax.axis_index("head")
    core = lax.rem(me, 2)
    chip = lax.div(me, 2)
    chip_x = lax.rem(chip, n_x)
    chip_y = lax.div(chip, n_x)
    sibling = chip * 2 + 1 - core

    def ahead(t):
        return lax.rem(chip_y + lax.div(t, n_x), n_y) * n_x + lax.rem(chip_x + lax.rem(t, n_x), n_x)

    def behind(t):
        return lax.rem(chip_y + n_y - lax.div(t, n_x), n_y) * n_x + lax.rem(
            chip_x + n_x - lax.rem(t, n_x), n_x
        )

    def nearest(t):
        value = ORDER[0] + 0 * t
        for k in range(1, n_chip):
            value = value + (ORDER[k] - ORDER[k - 1]) * lax.div(t + n_chip - k, n_chip)
        return value

    def mixed(t):
        return ahead(nearest(lax.rem(n_chip - t, n_chip)))

    def remote(src, dst, send, recv, head, pipe=None):
        return pltpu.make_async_remote_copy(
            src_ref=src,
            dst_ref=dst,
            send_sem=send,
            recv_sem=recv,
            device_id={"pipe": z if pipe is None else pipe, "head": head},
            device_id_type=MESH,
        )

    def drain(ref, sem):
        pltpu.make_async_copy(ref, ref, sem).wait()

    def each(first, last, body):
        def step(t, carry):
            body(t)
            return carry

        lax.fori_loop(first, last, step, 0)

    small = (
        (gain_in, gain),
        (dt_bias_in, dt_bias),
        (a_rate_in, a_rate),
        (d_skip_in, d_skip),
        (conv_x_in, conv_x),
        (conv_bc_in, conv_bc),
        (tail_x_in, tail_x),
        (tail_bc_in, tail_bc),
        (w_dt, wdt_v),
        (ssm_in, ssm_v),
    )
    for k, (src, dst) in enumerate(small):
        pltpu.make_async_copy(src, dst, load_sem.at[3 + k]).start()

    barrier = pltpu.get_barrier_semaphore()

    def greet(t):
        pl.semaphore_signal(
            barrier,
            inc=1,
            device_id={"pipe": z, "head": lax.rem(me + t, n_head)},
            device_id_type=MESH,
        )

    each(1, n_head, greet)
    for other in (lax.rem(z + 1, n_pipe), lax.rem(z + n_pipe - 1, n_pipe)):
        pl.semaphore_signal(
            barrier, inc=1, device_id={"pipe": other, "head": me}, device_id_type=MESH
        )
    def load_in(k):
        pltpu.make_async_copy(w_x.at[k], wx_v.at[k], load_sem.at[0]).start()
        pltpu.make_async_copy(w_bc.at[k], wbd_v.at[k, :, pl.ds(0, bc_cols)], load_sem.at[1]).start()

    each(0, n_chip, load_in)

    pl.semaphore_wait(barrier, n_head + 1)

    def turn(m):
        def give(t):
            to = lax.rem(me + t, n_head)
            remote(
                hid.at[m, :, pl.ds(pl.multiple_of(to * chunk, chunk), chunk)],
                first_in.at[m, me],
                first_s.at[m],
                first_r.at[m],
                to,
            ).start()

        each(1, n_head, give)
        pltpu.make_async_copy(
            hid.at[m, :, pl.ds(pl.multiple_of(me * chunk, chunk), chunk)],
            first_in.at[m, me],
            first_o.at[m],
        ).start()

    def spread(m):
        mine = h_all.at[m, me]

        for u in NEAR:
            remote(mine, mine, ag_s.at[m], ag_r.at[m, u], ahead(u) * 2 + core).start()
        remote(mine, mine, ag_s.at[m], fwd_r.at[m, 0], sibling).start()

    def begin(m):
        drain(first_in.at[m, 0], first_o.at[m])
        drain(first_in.at[m, pl.ds(0, n_head - 1)], first_r.at[m])
        for i in range(n_head):
            total[pl.ds(i * rows, rows), :] = first_in[m, i].astype(F32)
        h_all[m, me] = total[...].astype(BF16)
        spread(m)

    @pl.when(z == 0)
    def _():
        turn(0)

    for k, (src, dst) in enumerate(small):
        drain(dst, load_sem.at[3 + k])

    bc_all = conv_bc.shape[1]
    wide_k = 128 * GROUPS
    spans = bc_all // wide_k
    bc_rows[...] = jnp.zeros_like(bc_rows)
    bc_rows[0:4, :] = conv_bc[...]
    for k in range(3):
        bc_rows[4 + k : 5 + k, :] = tail_bc[k]
    pick_row = lax.broadcasted_iota(jnp.int32, (wide_k, 128), 0)
    pick_col = lax.broadcasted_iota(jnp.int32, (wide_k, 128), 1)
    pick = jnp.where(pick_row == pick_col * GROUPS + lax.div(me, per_group), 1.0, 0.0)
    spread_rows = jnp.concatenate(
        [bc_rows[:, k * wide_k : (k + 1) * wide_k] for k in range(spans)], axis=0
    )
    picked = exact(spread_rows, pick)
    taps[0:4, 0:inner] = conv_x[...]
    for k in range(3):
        taps[4 + k : 5 + k, 0:inner] = tail_x[k]
    for k in range(spans):
        taps[:, inner + k * 128 : inner + (k + 1) * 128] = picked[k * 8 : (k + 1) * 8]
    padded[5:8, :] = taps[4:7, :]

    ssm_t[...] = ssm_v[...].reshape(heads * HEAD_DIM, STATE).T

    @pl.when(z == 0)
    def _():
        begin(0)
        for m in range(1, micro):
            turn(m)

    dt_f = wdt_v[...].astype(F32)
    dt_cols = (
        jnp.concatenate([dt_f[:, k * 2 * chunk : (k + 1) * 2 * chunk] for k in range(n_chip)], axis=0)
        .T.astype(BF16)
        .astype(F32)
    )
    dt_at = lax.div(lax.broadcasted_iota(jnp.int32, dt_cols.shape, 1), heads)

    def join(k):
        wbd_v[k, :, bc_cols : bc_cols + 128] = jnp.where(dt_at == k, dt_cols, 0.0).astype(BF16)

    each(0, n_chip, join)

    for k in range(n_head):
        pltpu.make_async_copy(
            w_out.at[:, pl.ds(k * chunk, chunk)], wo_v.at[k], load_sem.at[2]
        ).start()
    drain(wx_v, load_sem.at[0])
    drain(wbd_v.at[:, :, pl.ds(0, bc_cols)], load_sem.at[1])

    def carry_on(m):
        remote(passed.at[m], h_all.at[m, me], pass_s, pass_r.at[m], me).wait_recv()
        spread(m)

    @pl.when(z > 0)
    def _():
        carry_on(0)

    def block(m):
        more = m < micro - 1

        acc[...] = jnp.zeros_like(acc)
        squares[...] = jnp.zeros_like(squares)

        def relay(u, handed=()):
            got = h_all.at[m, behind(u) * 2 + core]
            copy = remote(got, got, ag_s.at[m], ag_r.at[m, u], sibling)
            copy.wait_recv()
            for v in handed:
                remote(got, got, ag_s.at[m], ag_r.at[m, u + v], ahead(v) * 2 + core).start()
            remote(got, got, ag_s.at[m], fwd_r.at[m, u], sibling).start()

        for u in ORDER[1:EARLY]:
            relay(u, HANDED.get(u, ()))

        def project(t):
            @pl.when(jnp.logical_and(t + AHEAD >= EARLY, t + AHEAD < n_chip))
            def _():
                relay(nearest(t + AHEAD))

            u = nearest(t)
            src = behind(u)
            theirs = h_all.at[m, src * 2 + 1 - core]
            remote(theirs, theirs, ag_s.at[m], fwd_r.at[m, u], sibling).wait_recv()
            values = jnp.concatenate([h_all[m, src * 2], h_all[m, src * 2 + 1]], axis=1).astype(F32)
            sq = values * values
            part = sq[:, 0:128]
            for k in range(1, 2 * chunk // 128):
                part = part + sq[:, k * 128 : (k + 1) * 128]
            squares[...] += part
            scaled = (values * gain[src]).astype(BF16)
            acc[:, inner : inner + 256] += dot(scaled, wbd_v[src])
            return scaled

        def project_both(t):
            acc[:, 0:inner] += dot(project(t), wx_v[behind(nearest(t))])

        def project_later(t):
            scaled_v[t] = project(t)

        each(0, BEFORE, project_both)
        each(BEFORE, n_chip, project_later)
        inv = lax.rsqrt(jnp.sum(squares[...], axis=1, keepdims=True) / width + 1e-05)

        bc_dt = acc[:, inner : inner + 256] * inv
        bc_bf = bc_dt[:, 0:bc_cols].astype(BF16)
        bc_wide = jnp.concatenate([bc_bf, jnp.zeros((128 - tokens, bc_cols), BF16)], axis=0)
        at_row = lax.broadcasted_iota(jnp.int32, (bc_cols, bc_cols), 0)
        at_col = lax.broadcasted_iota(jnp.int32, (bc_cols, bc_cols), 1)
        width_n = bc_cols // GROUPS
        wanted = lax.rem(at_row, width_n) * GROUPS + lax.div(at_row, width_n)
        order = jnp.where(at_col == wanted, 1.0, 0.0).astype(BF16)
        bc_send[m] = dot(order, bc_wide, ((1,), (1,))).astype(BF16).reshape(bc_send.shape[1:])

        def give_bc(to):
            remote(
                bc_send.at[m, lax.div(to, per_group)], bc_recv.at[m, me], bc_s, bc_r.at[m], to
            ).start()

        def give_chip(t):
            to = mixed(t) * 2
            give_bc(to + core)
            give_bc(to + 1 - core)

        each(1, n_chip, give_chip)
        give_bc(sibling)
        bc_recv[m, me] = bc_send[m, lax.div(me, per_group)]

        @pl.when(jnp.logical_and(z == 0, more))
        def _():
            begin(m + 1)


        def finish(t):
            acc[:, 0:inner] += dot(scaled_v[t], wx_v[behind(nearest(t))])

        each(BEFORE, n_chip, finish)
        padded[8 : 8 + tokens, 0:inner] = acc[:, 0:inner] * inv

        def conv(lo, hi):
            summed = taps[0:1, lo:hi] * padded[5 : 5 + tokens, lo:hi]
            for k in range(1, 4):
                summed = summed + taps[k : k + 1, lo:hi] * padded[5 + k : 5 + k + tokens, lo:hi]
            return summed * lax.logistic(summed)

        x = conv(0, inner)
        fold_row = lax.broadcasted_iota(jnp.int32, (128, heads), 0)
        fold_col = lax.broadcasted_iota(jnp.int32, (128, heads), 1)
        fold = jnp.where(lax.rem(fold_row, heads) == fold_col, 1.0, 0.0)
        raw = exact(bc_dt[:, bc_cols : bc_cols + 128], fold) + dt_bias[...]
        step = jnp.maximum(raw, 0.0) + jnp.log1p(jnp.exp(-jnp.abs(raw)))
        tri_row = lax.broadcasted_iota(jnp.int32, (tokens, tokens), 0)
        tri_col = lax.broadcasted_iota(jnp.int32, (tokens, tokens), 1)
        log_decay = exact(jnp.where(tri_row >= tri_col, 1.0, 0.0), -step * a_rate[...])
        head_row = lax.broadcasted_iota(jnp.int32, (heads, inner), 0)
        head_col = lax.div(lax.broadcasted_iota(jnp.int32, (heads, inner), 1), HEAD_DIM)
        of_head = jnp.where(head_row == head_col, 1.0, 0.0)
        skip8 = jnp.broadcast_to(d_skip[...], (8, heads))
        wide = exact(jnp.concatenate([step, log_decay, skip8], axis=0), of_head)
        step_w = wide[0:tokens]
        log_w = wide[tokens : 2 * tokens]
        skip_w = wide[2 * tokens : 2 * tokens + 1]
        at_t = lax.broadcasted_iota(jnp.int32, (tokens, inner), 0)
        at_s = lax.rem(lax.broadcasted_iota(jnp.int32, (tokens, inner), 1), HEAD_DIM)
        log_s = jnp.sum(jnp.where(at_t == at_s, log_w, 0.0), axis=0, keepdims=True)
        causal = at_t >= at_s
        pair = jnp.where(causal, jnp.exp(jnp.where(causal, log_w - log_s, 0.0)), 0.0)
        log_end = log_w[tokens - 1 : tokens]
        x_dt = x * step_w
        x_end[...] = (jnp.exp(log_end - log_w) * x_dt).astype(BF16)
        decay_end[0:1, :] = jnp.exp(log_end)

        drain(bc_recv.at[m, pl.ds(0, n_head - 1)], bc_r.at[m])
        both = bc_recv[m].reshape(2 * STATE, 128).astype(F32).T
        padded[8 : 8 + tokens, inner : inner + 2 * STATE] = both[0:tokens]
        bc = conv(inner, inner + 2 * STATE)
        padded[5:8, :] = padded[5 + tokens : 8 + tokens, :]
        b_v = bc[:, 0:STATE].astype(BF16)
        c_v = bc[:, STATE : 2 * STATE].astype(BF16)
        b_end[...] = b_v
        scores = dot(c_v, jnp.concatenate([b_v, b_v], axis=0), ((1,), (1,)))
        weight = (jnp.concatenate([scores] * (heads // 2), axis=1) * pair).astype(BF16)
        lane = lax.broadcasted_iota(jnp.int32, (tokens, 2 * HEAD_DIM), 1)
        within = []
        for k in range(heads // 2):
            cols = slice(k * 2 * HEAD_DIM, (k + 1) * 2 * HEAD_DIM)
            two = x_dt[:, cols]
            stacked = jnp.concatenate(
                [jnp.where(lane < HEAD_DIM, two, 0.0), jnp.where(lane < HEAD_DIM, 0.0, two)], axis=0
            ).astype(BF16)
            within.append(dot(weight[:, cols], stacked))
        carried = jnp.exp(log_w) * dot(c_v, ssm_t[...].astype(BF16))
        y_v[...] = (jnp.concatenate(within, axis=1) + carried + skip_w * x).astype(BF16)

        @pl.when(m == 0)
        def _():
            drain(wo_v, load_sem.at[2])

        def for_sibling(i):
            t = lax.rem(i + 1, n_chip)
            sib_send[m, t] = dot(y_v[...], wo_v[mixed(t) * 2 + 1 - core]).astype(BF16)
            remote(sib_send.at[m, t], sib_recv.at[m, t], sib_s, sib_r.at[m, t], sibling).start()

        def product(t):
            return dot(y_v[...], wo_v[mixed(t) * 2 + core]).astype(BF16).astype(F32)

        def chip_sum(t, part):
            remote(
                sib_send.at[m, t], sib_recv.at[m, t], sib_s, sib_r.at[m, t], sibling
            ).wait_recv()
            return part + sib_recv[m, t].astype(F32)

        def for_owner(t, part):
            sum_send[m, t] = chip_sum(t, part).astype(BF16)
            remote(
                sum_send.at[m, t],
                sum_recv.at[m, t],
                sum_s,
                sum_r.at[m, t],
                mixed(t) * 2 + core,
            ).start()

        def for_both(i):
            part = product(i + 1)
            for_sibling(i + LEAD)
            for_owner(i + 1, part)

        each(0, LEAD, for_sibling)
        each(0, n_chip - LEAD, for_both)
        for t in range(n_chip - LEAD + 1, n_chip):
            for_owner(t, product(t))
        total[...] = chip_sum(0, product(0)) + h_all[m, me].astype(F32)

        ssm_t[...] = decay_end[0:1, :] * ssm_t[...] + dot(b_end[...], x_end[...], ((0,), (0,)))

        @pl.when(m == micro - 1)
        def _():
            state[...] = ssm_t[...].T.reshape(state.shape)

        def take(t):
            remote(
                sum_send.at[m, t], sum_recv.at[m, t], sum_s, sum_r.at[m, t], sibling
            ).wait_recv()
            total[...] += sum_recv[m, t].astype(F32)

        each(1, n_chip - 5, take)
        @pl.when(jnp.logical_and(z > 0, more))
        def _():
            carry_on(m + 1)

        each(n_chip - 5, n_chip, take)
        passed[m] = total[...].astype(BF16)

        @pl.when(z < n_pipe - 1)
        def _():
            remote(passed.at[m], h_all.at[m, me], pass_s, pass_r.at[m], me, z + 1).start()

        for i in range(n_head):
            out_send[m, i] = total[pl.ds(i * rows, rows), :].astype(BF16)

        def give_out(to):
            remote(
                out_send.at[m, to],
                out.at[m, :, pl.ds(pl.multiple_of(me * chunk, chunk), chunk)],
                out_s,
                out_r.at[m],
                to,
            ).start()

        def give_out_chip(t):
            to = mixed(t) * 2
            give_out(to + core)
            give_out(to + 1 - core)

        each(1, n_chip, give_out_chip)
        give_out(sibling)
        pltpu.make_async_copy(
            out_send.at[m, me],
            out.at[m, :, pl.ds(pl.multiple_of(me * chunk, chunk), chunk)],
            own_s.at[m],
        ).start()

    each(0, micro, block)
    def settle(m):
        drain(out_send.at[m, 0], own_s.at[m])
        drain(h_all.at[m, pl.ds(0, n_head - 1)], ag_s.at[m])
        drain(bc_recv.at[m, pl.ds(0, n_head - 1)], bc_s)
        drain(sib_send.at[m], sib_s)
        drain(sum_send.at[m, pl.ds(1, n_chip - 1)], sum_s)
        drain(out_send.at[m, pl.ds(0, n_head - 1)], out_s)

        @pl.when(z < n_pipe - 1)
        def _():
            drain(passed.at[m], pass_s)

        @pl.when(z == 0)
        def _():
            drain(first_in.at[m, pl.ds(0, n_head - 1)], first_s.at[m])

        drain(out.at[m, :, pl.ds(0, (n_head - 1) * chunk)], out_r.at[m])

    each(0, micro, settle)


def per_device(
    sizes,
    hidden,
    norm_gain,
    w_x,
    w_bc,
    w_dt,
    conv_x,
    conv_bc,
    dt_bias,
    a_rate,
    d_skip,
    w_out,
    ssm_init,
    conv_x_init,
    conv_bc_init,
):
    n_pipe, n_head, n_x, n_y = sizes
    n_chip = n_head // 2
    micro, rows, width = hidden.shape
    tokens = rows * n_head
    chunk = width // n_head
    inner = w_x.shape[2]
    heads = dt_bias.shape[1]
    bc_cols = w_bc.shape[2]
    vmem = pl.BlockSpec(memory_space=pltpu.VMEM)
    far = pl.BlockSpec(memory_space=pltpu.HBM)
    dma = pltpu.SemaphoreType.DMA
    out, state = pl.pallas_call(
        functools.partial(section, sizes),
        out_shape=(
            jax.ShapeDtypeStruct((micro, rows, width), BF16),
            jax.ShapeDtypeStruct(ssm_init.shape[1:], F32),
        ),
        in_specs=[far] * 14,
        out_specs=(vmem, vmem),
        scratch_shapes=[
            pltpu.VMEM((n_chip, 1, 2 * chunk), F32),
            pltpu.VMEM((1, heads), F32),
            pltpu.VMEM((1, heads), F32),
            pltpu.VMEM((1, heads), F32),
            pltpu.VMEM(conv_x.shape[1:], F32),
            pltpu.VMEM(conv_bc.shape[1:], F32),
            pltpu.VMEM((conv_x_init.shape[1], 1, conv_x_init.shape[2]), F32),
            pltpu.VMEM((conv_bc_init.shape[1], 1, conv_bc_init.shape[2]), F32),
            pltpu.VMEM((8, conv_bc.shape[2]), F32),
            pltpu.VMEM((8, inner + 2 * STATE), F32),
            pltpu.VMEM((n_chip, tokens, 2 * chunk), BF16),
            pltpu.VMEM((n_chip, 2 * chunk, inner), BF16),
            pltpu.VMEM((n_chip, 2 * chunk, 256), BF16),
            pltpu.VMEM((heads, width), BF16),
            pltpu.VMEM((n_head, inner, chunk), BF16),
            pltpu.VMEM(ssm_init.shape[1:], F32),
            pltpu.VMEM((STATE, inner), F32),
            pltpu.VMEM((micro, n_head, tokens, chunk), BF16),
            pltpu.VMEM((micro, n_head, rows, chunk), BF16),
            pltpu.VMEM((tokens, inner + 256), F32),
            pltpu.VMEM((tokens, 128), F32),
            pltpu.VMEM((8 + tokens, inner + 2 * STATE), F32),
            pltpu.VMEM((micro, GROUPS, bc_cols // GROUPS, 128), BF16),
            pltpu.VMEM((micro, n_head, bc_cols // GROUPS, 128), BF16),
            pltpu.VMEM((tokens, inner), BF16),
            pltpu.VMEM((tokens, inner), BF16),
            pltpu.VMEM((tokens, STATE), BF16),
            pltpu.VMEM((8, inner), F32),
            pltpu.VMEM((micro, n_chip, tokens, chunk), BF16),
            pltpu.VMEM((micro, n_chip, tokens, chunk), BF16),
            pltpu.VMEM((micro, n_chip, tokens, chunk), BF16),
            pltpu.VMEM((micro, n_chip, tokens, chunk), BF16),
            pltpu.VMEM((tokens, chunk), F32),
            pltpu.VMEM((micro, tokens, chunk), BF16),
            pltpu.VMEM((micro, n_head, rows, chunk), BF16),
            dma((13,)),
            dma((micro,)),
            dma((micro,)),
            dma((micro,)),
            dma((micro, n_chip)),
            dma((micro, n_chip)),
            dma,
            dma((micro,)),
            dma,
            dma((micro, n_chip)),
            dma,
            dma((micro, n_chip)),
            dma,
            dma((micro,)),
            dma,
            dma((micro,)),
            dma((micro,)),
            dma((micro,)),
        ],
        compiler_params=pltpu.CompilerParams(
            collective_id=0, has_side_effects=True, vmem_limit_bytes=48 << 20
        ),
    )(
        *(
            pltpu.with_memory_space_constraint(value, pltpu.HBM)
            for value in (
                hidden,
                w_x.reshape(n_chip, 2 * chunk, inner),
                w_bc.reshape(n_chip, 2 * chunk, bc_cols),
                w_dt[0].T,
                w_out[0],
                ssm_init[0],
                conv_x[0],
                conv_bc[0],
                conv_x_init.transpose(1, 0, 2),
                conv_bc_init.transpose(1, 0, 2),
                dt_bias,
                a_rate,
                d_skip,
                norm_gain.reshape(n_chip, 1, 2 * chunk),
            )
        )
    )
    return (out[None], state[None])


def solution(mesh):
    n_pipe = mesh.shape["pipe"]
    n_head = mesh.shape["head"]
    n_x = SIDE
    in_specs = (
        P(None, "head", None),
        P("pipe", None),
        P("pipe", None, "head"),
        P("pipe", None, "head"),
        P("pipe", None, "head"),
        P("pipe", None, "head"),
        P("pipe", None, None),
        P("pipe", "head"),
        P("pipe", "head"),
        P("pipe", "head"),
        P("pipe", "head", None),
        P("pipe", "head", None, None),
        P("pipe", None, "head"),
        P("pipe", None, None),
    )
    out_specs = (P("pipe", None, "head", None), P("pipe", "head", None, None))
    return jax.shard_map(
        functools.partial(per_device, (n_pipe, n_head, n_x, n_head // 2 // n_x)),
        mesh=mesh,
        in_specs=in_specs,
        out_specs=out_specs,
        check_vma=False,
    )
```

```python
import functools

import jax
import jax.numpy as jnp
from jax import lax
from jax.experimental import pallas as pl
from jax.experimental.pallas import tpu as pltpu
from jax.sharding import PartitionSpec as P

GROUPS = 8
STATE = 256
HEAD_DIM = 64
MESH = pl.DeviceIdType.MESH
F32 = jnp.float32
BF16 = jnp.bfloat16
AHEAD = 4
EARLY = 7
BEFORE = 6
LEAD = 4
SIDE = 4
NEAR = (2, 8, 1, 4, 3, 12, 5, 7, 13, 15)
ORDER = (0, 2, 8, 1, 4, 3, 12, 5, 7, 13, 15, 6, 14, 9, 11, 10)
HANDED = {2: (4, 12, 8), 8: (1, 3)}


def dot(a, b, dims=((1,), (0,)), precision=None):
    return lax.dot_general(a, b, (dims, ((), ())), precision=precision, preferred_element_type=F32)


def exact(a, b):
    return dot(a, b, precision=lax.Precision.HIGHEST)


def section(
    sizes,
    hid,
    w_x,
    w_bc,
    w_dt,
    w_out,
    ssm_in,
    conv_x_in,
    conv_bc_in,
    tail_x_in,
    tail_bc_in,
    dt_bias_in,
    a_rate_in,
    d_skip_in,
    gain_in,
    out,
    state,
    gain,
    dt_bias,
    a_rate,
    d_skip,
    conv_x,
    conv_bc,
    tail_x,
    tail_bc,
    bc_rows,
    taps,
    scaled_v,
    wx_v,
    wbd_v,
    wdt_v,
    wo_v,
    ssm_v,
    ssm_t,
    h_all,
    first_in,
    acc,
    squares,
    padded,
    bc_send,
    bc_recv,
    y_v,
    x_end,
    b_end,
    decay_end,
    sib_send,
    sib_recv,
    sum_send,
    sum_recv,
    total,
    passed,
    out_send,
    load_sem,
    first_s,
    first_r,
    ag_s,
    ag_r,
    fwd_r,
    bc_s,
    bc_r,
    sib_s,
    sib_r,
    sum_s,
    sum_r,
    pass_s,
    pass_r,
    out_s,
    out_r,
    own_s,
    first_o,
):
    n_pipe, n_head, n_x, n_y = sizes
    n_chip = n_head // 2
    micro = hid.shape[0]
    rows = hid.shape[1]
    width = hid.shape[2]
    tokens = rows * n_head
    chunk = width // n_head
    inner = w_x.shape[2]
    heads = dt_bias.shape[1]
    bc_cols = w_bc.shape[2]
    per_group = n_head // GROUPS
    z = lax.axis_index("pipe")
    me = lax.axis_index("head")
    core = lax.rem(me, 2)
    chip = lax.div(me, 2)
    chip_x = lax.rem(chip, n_x)
    chip_y = lax.div(chip, n_x)
    sibling = chip * 2 + 1 - core

    def ahead(t):
        return lax.rem(chip_y + lax.div(t, n_x), n_y) * n_x + lax.rem(chip_x + lax.rem(t, n_x), n_x)

    def behind(t):
        return lax.rem(chip_y + n_y - lax.div(t, n_x), n_y) * n_x + lax.rem(
            chip_x + n_x - lax.rem(t, n_x), n_x
        )

    def nearest(t):
        value = ORDER[0] + 0 * t
        for k in range(1, n_chip):
            value = value + (ORDER[k] - ORDER[k - 1]) * lax.div(t + n_chip - k, n_chip)
        return value

    def mixed(t):
        return ahead(nearest(lax.rem(n_chip - t, n_chip)))

    def remote(src, dst, send, recv, head, pipe=None):
        return pltpu.make_async_remote_copy(
            src_ref=src,
            dst_ref=dst,
            send_sem=send,
            recv_sem=recv,
            device_id={"pipe": z if pipe is None else pipe, "head": head},
            device_id_type=MESH,
        )

    def drain(ref, sem):
        pltpu.make_async_copy(ref, ref, sem).wait()

    def each(first, last, body):
        def step(t, carry):
            body(t)
            return carry

        lax.fori_loop(first, last, step, 0)

    small = (
        (gain_in, gain),
        (dt_bias_in, dt_bias),
        (a_rate_in, a_rate),
        (d_skip_in, d_skip),
        (conv_x_in, conv_x),
        (conv_bc_in, conv_bc),
        (tail_x_in, tail_x),
        (tail_bc_in, tail_bc),
        (w_dt, wdt_v),
        (ssm_in, ssm_v),
    )
    for k, (src, dst) in enumerate(small):
        pltpu.make_async_copy(src, dst, load_sem.at[3 + k]).start()

    barrier = pltpu.get_barrier_semaphore()

    def greet(t):
        pl.semaphore_signal(
            barrier,
            inc=1,
            device_id={"pipe": z, "head": lax.rem(me + t, n_head)},
            device_id_type=MESH,
        )

    each(1, n_head, greet)
    for other in (lax.rem(z + 1, n_pipe), lax.rem(z + n_pipe - 1, n_pipe)):
        pl.semaphore_signal(
            barrier, inc=1, device_id={"pipe": other, "head": me}, device_id_type=MESH
        )
    def load_in(k):
        pltpu.make_async_copy(w_x.at[k], wx_v.at[k], load_sem.at[0]).start()
        pltpu.make_async_copy(w_bc.at[k], wbd_v.at[k, :, pl.ds(0, bc_cols)], load_sem.at[1]).start()

    each(0, n_chip, load_in)

    pl.semaphore_wait(barrier, n_head + 1)

    def turn(m):
        def give(t):
            to = lax.rem(me + t, n_head)
            remote(
                hid.at[m, :, pl.ds(pl.multiple_of(to * chunk, chunk), chunk)],
                first_in.at[m, me],
                first_s.at[m],
                first_r.at[m],
                to,
            ).start()

        each(1, n_head, give)
        pltpu.make_async_copy(
            hid.at[m, :, pl.ds(pl.multiple_of(me * chunk, chunk), chunk)],
            first_in.at[m, me],
            first_o.at[m],
        ).start()

    def spread(m):
        mine = h_all.at[m, me]

        for u in NEAR:
            remote(mine, mine, ag_s.at[m], ag_r.at[m, u], ahead(u) * 2 + core).start()
        remote(mine, mine, ag_s.at[m], fwd_r.at[m, 0], sibling).start()

    def begin(m):
        drain(first_in.at[m, 0], first_o.at[m])
        drain(first_in.at[m, pl.ds(0, n_head - 1)], first_r.at[m])
        for i in range(n_head):
            total[pl.ds(i * rows, rows), :] = first_in[m, i].astype(F32)
        h_all[m, me] = total[...].astype(BF16)
        spread(m)

    @pl.when(z == 0)
    def _():
        turn(0)

    for k, (src, dst) in enumerate(small):
        drain(dst, load_sem.at[3 + k])

    bc_all = conv_bc.shape[1]
    wide_k = 128 * GROUPS
    spans = bc_all // wide_k
    bc_rows[...] = jnp.zeros_like(bc_rows)
    bc_rows[0:4, :] = conv_bc[...]
    for k in range(3):
        bc_rows[4 + k : 5 + k, :] = tail_bc[k]
    pick_row = lax.broadcasted_iota(jnp.int32, (wide_k, 128), 0)
    pick_col = lax.broadcasted_iota(jnp.int32, (wide_k, 128), 1)
    pick = jnp.where(pick_row == pick_col * GROUPS + lax.div(me, per_group), 1.0, 0.0)
    spread_rows = jnp.concatenate(
        [bc_rows[:, k * wide_k : (k + 1) * wide_k] for k in range(spans)], axis=0
    )
    picked = exact(spread_rows, pick)
    taps[0:4, 0:inner] = conv_x[...]
    for k in range(3):
        taps[4 + k : 5 + k, 0:inner] = tail_x[k]
    for k in range(spans):
        taps[:, inner + k * 128 : inner + (k + 1) * 128] = picked[k * 8 : (k + 1) * 8]
    padded[5:8, :] = taps[4:7, :]

    ssm_t[...] = ssm_v[...].reshape(heads * HEAD_DIM, STATE).T

    @pl.when(z == 0)
    def _():
        begin(0)
        for m in range(1, micro):
            turn(m)

    dt_f = wdt_v[...].astype(F32)
    dt_cols = (
        jnp.concatenate([dt_f[:, k * 2 * chunk : (k + 1) * 2 * chunk] for k in range(n_chip)], axis=0)
        .T.astype(BF16)
        .astype(F32)
    )
    dt_at = lax.div(lax.broadcasted_iota(jnp.int32, dt_cols.shape, 1), heads)

    def join(k):
        wbd_v[k, :, bc_cols : bc_cols + 128] = jnp.where(dt_at == k, dt_cols, 0.0).astype(BF16)

    each(0, n_chip, join)

    for k in range(n_head):
        pltpu.make_async_copy(
            w_out.at[:, pl.ds(k * chunk, chunk)], wo_v.at[k], load_sem.at[2]
        ).start()
    drain(wx_v, load_sem.at[0])
    drain(wbd_v.at[:, :, pl.ds(0, bc_cols)], load_sem.at[1])

    def carry_on(m):
        remote(passed.at[m], h_all.at[m, me], pass_s, pass_r.at[m], me).wait_recv()
        spread(m)

    @pl.when(z > 0)
    def _():
        carry_on(0)

    def block(m):
        more = m < micro - 1

        acc[...] = jnp.zeros_like(acc)
        squares[...] = jnp.zeros_like(squares)

        def relay(u, handed=()):
            got = h_all.at[m, behind(u) * 2 + core]
            copy = remote(got, got, ag_s.at[m], ag_r.at[m, u], sibling)
            copy.wait_recv()
            for v in handed:
                remote(got, got, ag_s.at[m], ag_r.at[m, u + v], ahead(v) * 2 + core).start()
            remote(got, got, ag_s.at[m], fwd_r.at[m, u], sibling).start()

        for u in ORDER[1:EARLY]:
            relay(u, HANDED.get(u, ()))

        def project(t):
            @pl.when(jnp.logical_and(t + AHEAD >= EARLY, t + AHEAD < n_chip))
            def _():
                relay(nearest(t + AHEAD))

            u = nearest(t)
            src = behind(u)
            theirs = h_all.at[m, src * 2 + 1 - core]
            remote(theirs, theirs, ag_s.at[m], fwd_r.at[m, u], sibling).wait_recv()
            values = jnp.concatenate([h_all[m, src * 2], h_all[m, src * 2 + 1]], axis=1).astype(F32)
            sq = values * values
            part = sq[:, 0:128]
            for k in range(1, 2 * chunk // 128):
                part = part + sq[:, k * 128 : (k + 1) * 128]
            squares[...] += part
            scaled = (values * gain[src]).astype(BF16)
            acc[:, inner : inner + 256] += dot(scaled, wbd_v[src])
            return scaled

        def project_both(t):
            acc[:, 0:inner] += dot(project(t), wx_v[behind(nearest(t))])

        def project_later(t):
            scaled_v[t] = project(t)

        each(0, BEFORE, project_both)
        each(BEFORE, n_chip, project_later)
        inv = lax.rsqrt(jnp.sum(squares[...], axis=1, keepdims=True) / width + 1e-05)

        bc_dt = acc[:, inner : inner + 256] * inv
        bc_bf = bc_dt[:, 0:bc_cols].astype(BF16)
        bc_wide = jnp.concatenate([bc_bf, jnp.zeros((128 - tokens, bc_cols), BF16)], axis=0)
        at_row = lax.broadcasted_iota(jnp.int32, (bc_cols, bc_cols), 0)
        at_col = lax.broadcasted_iota(jnp.int32, (bc_cols, bc_cols), 1)
        width_n = bc_cols // GROUPS
        wanted = lax.rem(at_row, width_n) * GROUPS + lax.div(at_row, width_n)
        order = jnp.where(at_col == wanted, 1.0, 0.0).astype(BF16)
        bc_send[m] = dot(order, bc_wide, ((1,), (1,))).astype(BF16).reshape(bc_send.shape[1:])

        def give_bc(to):
            remote(
                bc_send.at[m, lax.div(to, per_group)], bc_recv.at[m, me], bc_s, bc_r.at[m], to
            ).start()

        def give_chip(t):
            to = mixed(t) * 2
            give_bc(to + core)
            give_bc(to + 1 - core)

        each(1, n_chip, give_chip)
        give_bc(sibling)
        bc_recv[m, me] = bc_send[m, lax.div(me, per_group)]

        @pl.when(jnp.logical_and(z == 0, more))
        def _():
            begin(m + 1)


        def finish(t):
            acc[:, 0:inner] += dot(scaled_v[t], wx_v[behind(nearest(t))])

        each(BEFORE, n_chip, finish)
        padded[8 : 8 + tokens, 0:inner] = acc[:, 0:inner] * inv

        def conv(lo, hi):
            summed = taps[0:1, lo:hi] * padded[5 : 5 + tokens, lo:hi]
            for k in range(1, 4):
                summed = summed + taps[k : k + 1, lo:hi] * padded[5 + k : 5 + k + tokens, lo:hi]
            return summed * lax.logistic(summed)

        x = conv(0, inner)
        fold_row = lax.broadcasted_iota(jnp.int32, (128, heads), 0)
        fold_col = lax.broadcasted_iota(jnp.int32, (128, heads), 1)
        fold = jnp.where(lax.rem(fold_row, heads) == fold_col, 1.0, 0.0)
        raw = exact(bc_dt[:, bc_cols : bc_cols + 128], fold) + dt_bias[...]
        step = jnp.maximum(raw, 0.0) + jnp.log1p(jnp.exp(-jnp.abs(raw)))
        tri_row = lax.broadcasted_iota(jnp.int32, (tokens, tokens), 0)
        tri_col = lax.broadcasted_iota(jnp.int32, (tokens, tokens), 1)
        log_decay = exact(jnp.where(tri_row >= tri_col, 1.0, 0.0), -step * a_rate[...])
        head_row = lax.broadcasted_iota(jnp.int32, (heads, inner), 0)
        head_col = lax.div(lax.broadcasted_iota(jnp.int32, (heads, inner), 1), HEAD_DIM)
        of_head = jnp.where(head_row == head_col, 1.0, 0.0)
        skip8 = jnp.broadcast_to(d_skip[...], (8, heads))
        wide = exact(jnp.concatenate([step, log_decay, skip8], axis=0), of_head)
        step_w = wide[0:tokens]
        log_w = wide[tokens : 2 * tokens]
        skip_w = wide[2 * tokens : 2 * tokens + 1]
        at_t = lax.broadcasted_iota(jnp.int32, (tokens, inner), 0)
        at_s = lax.rem(lax.broadcasted_iota(jnp.int32, (tokens, inner), 1), HEAD_DIM)
        log_s = jnp.sum(jnp.where(at_t == at_s, log_w, 0.0), axis=0, keepdims=True)
        causal = at_t >= at_s
        pair = jnp.where(causal, jnp.exp(jnp.where(causal, log_w - log_s, 0.0)), 0.0)
        log_end = log_w[tokens - 1 : tokens]
        x_dt = x * step_w
        x_end[...] = (jnp.exp(log_end - log_w) * x_dt).astype(BF16)
        decay_end[0:1, :] = jnp.exp(log_end)

        drain(bc_recv.at[m, pl.ds(0, n_head - 1)], bc_r.at[m])
        both = bc_recv[m].reshape(2 * STATE, 128).astype(F32).T
        padded[8 : 8 + tokens, inner : inner + 2 * STATE] = both[0:tokens]
        bc = conv(inner, inner + 2 * STATE)
        padded[5:8, :] = padded[5 + tokens : 8 + tokens, :]
        b_v = bc[:, 0:STATE].astype(BF16)
        c_v = bc[:, STATE : 2 * STATE].astype(BF16)
        b_end[...] = b_v
        scores = dot(c_v, jnp.concatenate([b_v, b_v], axis=0), ((1,), (1,)))
        weight = (jnp.concatenate([scores] * (heads // 2), axis=1) * pair).astype(BF16)
        lane = lax.broadcasted_iota(jnp.int32, (tokens, 2 * HEAD_DIM), 1)
        within = []
        for k in range(heads // 2):
            cols = slice(k * 2 * HEAD_DIM, (k + 1) * 2 * HEAD_DIM)
            two = x_dt[:, cols]
            stacked = jnp.concatenate(
                [jnp.where(lane < HEAD_DIM, two, 0.0), jnp.where(lane < HEAD_DIM, 0.0, two)], axis=0
            ).astype(BF16)
            within.append(dot(weight[:, cols], stacked))
        carried = jnp.exp(log_w) * dot(c_v, ssm_t[...].astype(BF16))
        y_v[...] = (jnp.concatenate(within, axis=1) + carried + skip_w * x).astype(BF16)

        @pl.when(m == 0)
        def _():
            drain(wo_v, load_sem.at[2])

        def for_sibling(i):
            t = lax.rem(i + 1, n_chip)
            sib_send[m, t] = dot(y_v[...], wo_v[mixed(t) * 2 + 1 - core]).astype(BF16)
            remote(sib_send.at[m, t], sib_recv.at[m, t], sib_s, sib_r.at[m, t], sibling).start()

        def product(t):
            return dot(y_v[...], wo_v[mixed(t) * 2 + core]).astype(BF16).astype(F32)

        def chip_sum(t, part):
            remote(
                sib_send.at[m, t], sib_recv.at[m, t], sib_s, sib_r.at[m, t], sibling
            ).wait_recv()
            return part + sib_recv[m, t].astype(F32)

        def for_owner(t, part):
            sum_send[m, t] = chip_sum(t, part).astype(BF16)
            remote(
                sum_send.at[m, t],
                sum_recv.at[m, t],
                sum_s,
                sum_r.at[m, t],
                mixed(t) * 2 + core,
            ).start()

        def for_both(i):
            part = product(i + 1)
            for_sibling(i + LEAD)
            for_owner(i + 1, part)

        each(0, LEAD, for_sibling)
        each(0, n_chip - LEAD, for_both)
        for t in range(n_chip - LEAD + 1, n_chip):
            for_owner(t, product(t))
        total[...] = chip_sum(0, product(0)) + h_all[m, me].astype(F32)

        ssm_t[...] = decay_end[0:1, :] * ssm_t[...] + dot(b_end[...], x_end[...], ((0,), (0,)))

        @pl.when(m == micro - 1)
        def _():
            state[...] = ssm_t[...].T.reshape(state.shape)

        def take(t):
            remote(
                sum_send.at[m, t], sum_recv.at[m, t], sum_s, sum_r.at[m, t], sibling
            ).wait_recv()
            total[...] += sum_recv[m, t].astype(F32)

        each(1, n_chip - 8, take)
        @pl.when(jnp.logical_and(z > 0, more))
        def _():
            carry_on(m + 1)

        each(n_chip - 8, n_chip, take)
        passed[m] = total[...].astype(BF16)

        @pl.when(z < n_pipe - 1)
        def _():
            remote(passed.at[m], h_all.at[m, me], pass_s, pass_r.at[m], me, z + 1).start()

        for i in range(n_head):
            out_send[m, i] = total[pl.ds(i * rows, rows), :].astype(BF16)

        def give_out(to):
            remote(
                out_send.at[m, to],
                out.at[m, :, pl.ds(pl.multiple_of(me * chunk, chunk), chunk)],
                out_s,
                out_r.at[m],
                to,
            ).start()

        def give_out_chip(t):
            to = mixed(t) * 2
            give_out(to + core)
            give_out(to + 1 - core)

        each(1, n_chip, give_out_chip)
        give_out(sibling)
        pltpu.make_async_copy(
            out_send.at[m, me],
            out.at[m, :, pl.ds(pl.multiple_of(me * chunk, chunk), chunk)],
            own_s.at[m],
        ).start()

    each(0, micro, block)
    def settle(m):
        drain(out_send.at[m, 0], own_s.at[m])
        drain(h_all.at[m, pl.ds(0, n_head - 1)], ag_s.at[m])
        drain(bc_recv.at[m, pl.ds(0, n_head - 1)], bc_s)
        drain(sib_send.at[m], sib_s)
        drain(sum_send.at[m, pl.ds(1, n_chip - 1)], sum_s)
        drain(out_send.at[m, pl.ds(0, n_head - 1)], out_s)

        @pl.when(z < n_pipe - 1)
        def _():
            drain(passed.at[m], pass_s)

        @pl.when(z == 0)
        def _():
            drain(first_in.at[m, pl.ds(0, n_head - 1)], first_s.at[m])

        drain(out.at[m, :, pl.ds(0, (n_head - 1) * chunk)], out_r.at[m])

    each(0, micro, settle)


def per_device(
    sizes,
    hidden,
    norm_gain,
    w_x,
    w_bc,
    w_dt,
    conv_x,
    conv_bc,
    dt_bias,
    a_rate,
    d_skip,
    w_out,
    ssm_init,
    conv_x_init,
    conv_bc_init,
):
    n_pipe, n_head, n_x, n_y = sizes
    n_chip = n_head // 2
    micro, rows, width = hidden.shape
    tokens = rows * n_head
    chunk = width // n_head
    inner = w_x.shape[2]
    heads = dt_bias.shape[1]
    bc_cols = w_bc.shape[2]
    vmem = pl.BlockSpec(memory_space=pltpu.VMEM)
    far = pl.BlockSpec(memory_space=pltpu.HBM)
    dma = pltpu.SemaphoreType.DMA
    out, state = pl.pallas_call(
        functools.partial(section, sizes),
        out_shape=(
            jax.ShapeDtypeStruct((micro, rows, width), BF16),
            jax.ShapeDtypeStruct(ssm_init.shape[1:], F32),
        ),
        in_specs=[far] * 14,
        out_specs=(vmem, vmem),
        scratch_shapes=[
            pltpu.VMEM((n_chip, 1, 2 * chunk), F32),
            pltpu.VMEM((1, heads), F32),
            pltpu.VMEM((1, heads), F32),
            pltpu.VMEM((1, heads), F32),
            pltpu.VMEM(conv_x.shape[1:], F32),
            pltpu.VMEM(conv_bc.shape[1:], F32),
            pltpu.VMEM((conv_x_init.shape[1], 1, conv_x_init.shape[2]), F32),
            pltpu.VMEM((conv_bc_init.shape[1], 1, conv_bc_init.shape[2]), F32),
            pltpu.VMEM((8, conv_bc.shape[2]), F32),
            pltpu.VMEM((8, inner + 2 * STATE), F32),
            pltpu.VMEM((n_chip, tokens, 2 * chunk), BF16),
            pltpu.VMEM((n_chip, 2 * chunk, inner), BF16),
            pltpu.VMEM((n_chip, 2 * chunk, 256), BF16),
            pltpu.VMEM((heads, width), BF16),
            pltpu.VMEM((n_head, inner, chunk), BF16),
            pltpu.VMEM(ssm_init.shape[1:], F32),
            pltpu.VMEM((STATE, inner), F32),
            pltpu.VMEM((micro, n_head, tokens, chunk), BF16),
            pltpu.VMEM((micro, n_head, rows, chunk), BF16),
            pltpu.VMEM((tokens, inner + 256), F32),
            pltpu.VMEM((tokens, 128), F32),
            pltpu.VMEM((8 + tokens, inner + 2 * STATE), F32),
            pltpu.VMEM((micro, GROUPS, bc_cols // GROUPS, 128), BF16),
            pltpu.VMEM((micro, n_head, bc_cols // GROUPS, 128), BF16),
            pltpu.VMEM((tokens, inner), BF16),
            pltpu.VMEM((tokens, inner), BF16),
            pltpu.VMEM((tokens, STATE), BF16),
            pltpu.VMEM((8, inner), F32),
            pltpu.VMEM((micro, n_chip, tokens, chunk), BF16),
            pltpu.VMEM((micro, n_chip, tokens, chunk), BF16),
            pltpu.VMEM((micro, n_chip, tokens, chunk), BF16),
            pltpu.VMEM((micro, n_chip, tokens, chunk), BF16),
            pltpu.VMEM((tokens, chunk), F32),
            pltpu.VMEM((micro, tokens, chunk), BF16),
            pltpu.VMEM((micro, n_head, rows, chunk), BF16),
            dma((13,)),
            dma((micro,)),
            dma((micro,)),
            dma((micro,)),
            dma((micro, n_chip)),
            dma((micro, n_chip)),
            dma,
            dma((micro,)),
            dma,
            dma((micro, n_chip)),
            dma,
            dma((micro, n_chip)),
            dma,
            dma((micro,)),
            dma,
            dma((micro,)),
            dma((micro,)),
            dma((micro,)),
        ],
        compiler_params=pltpu.CompilerParams(
            collective_id=0, has_side_effects=True, vmem_limit_bytes=48 << 20
        ),
    )(
        *(
            pltpu.with_memory_space_constraint(value, pltpu.HBM)
            for value in (
                hidden,
                w_x.reshape(n_chip, 2 * chunk, inner),
                w_bc.reshape(n_chip, 2 * chunk, bc_cols),
                w_dt[0].T,
                w_out[0],
                ssm_init[0],
                conv_x[0],
                conv_bc[0],
                conv_x_init.transpose(1, 0, 2),
                conv_bc_init.transpose(1, 0, 2),
                dt_bias,
                a_rate,
                d_skip,
                norm_gain.reshape(n_chip, 1, 2 * chunk),
            )
        )
    )
    return (out[None], state[None])


def solution(mesh):
    n_pipe = mesh.shape["pipe"]
    n_head = mesh.shape["head"]
    n_x = SIDE
    in_specs = (
        P(None, "head", None),
        P("pipe", None),
        P("pipe", None, "head"),
        P("pipe", None, "head"),
        P("pipe", None, "head"),
        P("pipe", None, "head"),
        P("pipe", None, None),
        P("pipe", "head"),
        P("pipe", "head"),
        P("pipe", "head"),
        P("pipe", "head", None),
        P("pipe", "head", None, None),
        P("pipe", None, "head"),
        P("pipe", None, None),
    )
    out_specs = (P("pipe", None, "head", None), P("pipe", "head", None, None))
    return jax.shard_map(
        functools.partial(per_device, (n_pipe, n_head, n_x, n_head // 2 // n_x)),
        mesh=mesh,
        in_specs=in_specs,
        out_specs=out_specs,
        check_vma=False,
    )
```
